32 devices in a mesh: segment: 8 (over z, x), tp: 4 (over y, core).
Axes of the slice: x: 2, y: 2, z: 4, core: 2. Of those that a mesh axis runs over, the one named last changes fastest.
Arguments:
- layer_inputs: bfloat16 [8, 2, 128, 2048], P('segment', None, 'tp'), may hold values from -100 to 100, as said below
- cotangent: bfloat16 [2, 2, 128, 2048], P(None, None, 'tp'), may hold values from -6 to 6
- gate_weight: bfloat16 [8, 2048, 4096], P('segment', None, 'tp'), may hold values from -1 to 1, as said below
- up_weight: bfloat16 [8, 2048, 4096], P('segment', None, 'tp'), may hold values from -1 to 1, as said below
- down_weight: bfloat16 [8, 4096, 2048], P('segment', 'tp'), may hold values from -1 to 1, as said below
- gate_momentum: float32 [8, 1024, 4096], P('segment', None, 'tp'), may hold values from -48 to 48
- up_momentum: float32 [8, 1024, 4096], P('segment', None, 'tp'), may hold values from -48 to 48
- down_momentum: float32 [8, 4096, 1024], P('segment', 'tp'), may hold values from -48 to 48
Outputs:
- input_gradient: bfloat16 [8, 2, 128, 2048], P('segment', None, 'tp')
- new_gate_momentum: float32 [8, 1024, 4096], P('segment', None, 'tp')
- new_up_momentum: float32 [8, 1024, 4096], P('segment', None, 'tp')
- new_down_momentum: float32 [8, 4096, 1024], P('segment', 'tp')
The draws below stay inside these ranges and needn't reach their ends.
Inputs may be any that keep to these rules, and one draw needn't show every extreme that they name: `layer_inputs`: stored layer inputs, independent for every section and micro-batch. `gate_weight`: sections 2l and 2l + 1 hold equal copies of one layer's weights. `up_weight`: sections 2l and 2l + 1 hold equal copies of one layer's weights. `down_weight`: sections 2l and 2l + 1 hold equal copies of one layer's weights.
All inputs are finite; a program needn't handle non-finite values.
Results may differ from the reference program's by a relative error of at most 0.02.
Values may be sent and summed in bfloat16 or wider, within the bound.
A program may use at most 128 MiB of HBM per device.

```python
import math
import jax
import jax.numpy as jnp
from jax import lax

D = 2048
FF = 4096
ROWS = 128
MICRO = 2
LAYERS = 4
HALF = 1024
FF_DEV = 1024
N_TP = 4


def clipped_normal(key, shape):
    return jnp.clip(jax.random.normal(key, shape, jnp.float32), -4.0, 4.0)


def draw_layer_inputs(key, part):
    shape = (2 * LAYERS, MICRO, ROWS, D)
    noise_key, row_key, column_key = jax.random.split(jax.random.fold_in(key, 101), 3)
    noise = clipped_normal(noise_key, shape)
    row_scale = jnp.exp(jax.random.uniform(row_key, (2 * LAYERS, MICRO, ROWS, 1), jnp.float32, 0.0, math.log(10.0)))
    column_scale = jnp.exp(jax.random.uniform(column_key, (2 * LAYERS, MICRO, 1, D), jnp.float32, math.log(0.25), math.log(2.5)))
    return (noise * row_scale * column_scale).astype(jnp.bfloat16)


def mirrored(key, shape, fan_in):
    values = clipped_normal(key, shape)
    values = values * fan_in ** (-0.5)
    return jnp.repeat(values, 2, axis=0).astype(jnp.bfloat16)


def draw_gate_weight(key, part):
    return mirrored(jax.random.fold_in(key, 211), (LAYERS, D, FF), D)


def draw_up_weight(key, part):
    return mirrored(jax.random.fold_in(key, 223), (LAYERS, D, FF), D)


def draw_down_weight(key, part):
    return mirrored(jax.random.fold_in(key, 227), (LAYERS, FF, D), FF)


def block_levels(key, extent, cuts, low, largest):
    def one(dim, shards_of):
        steps = jax.random.uniform(jax.random.fold_in(jax.random.fold_in(key, 6), dim), (shards_of,), jnp.float32, low / len(cuts), largest / len(cuts))
        return jnp.repeat(jnp.exp(steps), extent[dim] // shards_of).reshape((-1,) + (1,) * (len(extent) - dim - 1))

    loudness = one(*cuts[0])
    for cut in cuts[1:]:
        loudness = loudness * one(*cut)
    return loudness


def centred(stream_key, extent, deviation, most, cuts=(), held_as=jnp.bfloat16):
    entries = deviation * jax.random.normal(stream_key, extent, jnp.float32)
    if cuts:
        entries = entries * block_levels(stream_key, extent, cuts, -0.22, 0.18)
    return jnp.clip(entries, -most, most).astype(held_as)


def setup_inputs(seed: int = 0) -> dict:
    key_list = jax.random.split(jax.random.key(seed), 9)
    layer_inputs = draw_layer_inputs(jax.random.fold_in(key_list[8], 71), 0)
    cotangent = centred(key_list[1], (2, MICRO, ROWS, D), 1.0, 6.0, ((2, 4),))
    gate_weight = draw_gate_weight(jax.random.fold_in(key_list[8], 71), 0)
    up_weight = draw_up_weight(jax.random.fold_in(key_list[8], 71), 0)
    down_weight = draw_down_weight(jax.random.fold_in(key_list[8], 71), 0)
    gate_momentum = centred(key_list[5], (2 * LAYERS, HALF, FF), 8.0, 48.0, ((0, 8), (2, 4)), jnp.float32)
    up_momentum = centred(key_list[6], (2 * LAYERS, HALF, FF), 8.0, 48.0, ((0, 8), (2, 4)), jnp.float32)
    down_momentum = centred(key_list[7], (2 * LAYERS, FF, HALF), 8.0, 48.0, ((0, 8), (1, 4)), jnp.float32)
    return dict(layer_inputs=layer_inputs, cotangent=cotangent, gate_weight=gate_weight, up_weight=up_weight, down_weight=down_weight, gate_momentum=gate_momentum, up_momentum=up_momentum, down_momentum=down_momentum)


epsilon = 1e-05
momentum_decay = 0.9

def rounded(values):
    return lax.optimization_barrier(values.astype(jnp.bfloat16)).astype(jnp.float32)

def section_backward(inputs, incoming, gate_weight, up_weight, down_weight):
    rows = inputs.reshape(-1, D).astype(jnp.float32)
    inverse_norm = lax.rsqrt(lax.optimization_barrier(jnp.mean(rows * rows, axis=-1, keepdims=True)) + epsilon)
    exact = rows * inverse_norm
    normed = exact.astype(jnp.bfloat16)
    gate = jnp.dot(normed, gate_weight, preferred_element_type=jnp.float32)
    up = jnp.dot(normed, up_weight, preferred_element_type=jnp.float32)
    sigma = jax.nn.sigmoid(gate)
    silu = gate * sigma
    hidden = (silu * up).astype(jnp.bfloat16)
    arriving = incoming.reshape(-1, D)
    hidden_grad = jnp.dot(arriving, down_weight.T, preferred_element_type=jnp.float32)
    gate_grad = (hidden_grad * up * sigma * (1.0 + gate * (1.0 - sigma))).astype(jnp.bfloat16)
    up_grad = (hidden_grad * silu).astype(jnp.bfloat16)
    gate_parts = jnp.einsum('rgf,dgf->grd', gate_grad.astype(jnp.float32).reshape(-1, N_TP, FF_DEV), gate_weight.astype(jnp.float32).reshape(D, N_TP, FF_DEV), precision=lax.Precision.HIGHEST)
    up_parts = jnp.einsum('rgf,dgf->grd', up_grad.astype(jnp.float32).reshape(-1, N_TP, FF_DEV), up_weight.astype(jnp.float32).reshape(D, N_TP, FF_DEV), precision=lax.Precision.HIGHEST)
    parts = lax.optimization_barrier((gate_parts + up_parts).astype(jnp.bfloat16))
    normed_grad = lax.optimization_barrier(jnp.sum(parts.astype(jnp.float32), axis=0))
    back = arriving.astype(jnp.float32) + inverse_norm * (normed_grad - exact * lax.optimization_barrier(jnp.mean(normed_grad * exact, axis=-1, keepdims=True)))
    back = back.astype(jnp.bfloat16).reshape(inputs.shape)
    weights = (jnp.dot(normed.T, gate_grad, preferred_element_type=jnp.float32), jnp.dot(normed.T, up_grad, preferred_element_type=jnp.float32), jnp.dot(hidden.T, arriving, preferred_element_type=jnp.float32))
    return (back, weights)

def reference(layer_inputs, cotangent, gate_weight, up_weight, down_weight, gate_momentum, up_momentum, down_momentum):

    def step(incoming, position):
        sections = (2 * position, 2 * position + 1)
        backs = []
        totals = []
        for direction in range(2):
            section = sections[direction]
            back, weights = section_backward(lax.dynamic_index_in_dim(layer_inputs, section, 0, False), incoming[direction], lax.dynamic_index_in_dim(gate_weight, section, 0, False), lax.dynamic_index_in_dim(up_weight, section, 0, False), lax.dynamic_index_in_dim(down_weight, section, 0, False))
            backs.append(back)
            totals.append(weights)
        lower_sum = [totals[0][which] + rounded(totals[1][which]) for which in range(3)]
        upper_sum = [totals[1][which] + rounded(totals[0][which]) for which in range(3)]
        lower = (momentum_decay * gate_momentum[sections[0]] + lower_sum[0][:HALF], momentum_decay * up_momentum[sections[0]] + lower_sum[1][:HALF], momentum_decay * down_momentum[sections[0]] + lower_sum[2][:, :HALF])
        upper = (momentum_decay * gate_momentum[sections[1]] + upper_sum[0][HALF:], momentum_decay * up_momentum[sections[1]] + upper_sum[1][HALF:], momentum_decay * down_momentum[sections[1]] + upper_sum[2][:, HALF:])
        stacked = jnp.stack(backs)
        return (stacked, (stacked, lower, upper))
    positions = jnp.arange(LAYERS, dtype=jnp.int32)
    _, (backs, lower, upper) = lax.scan(step, cotangent, positions)
    input_gradient = backs.reshape((2 * LAYERS,) + backs.shape[2:])
    results = []
    for which in range(3):
        paired = jnp.stack([lower[which], upper[which]], axis=1)
        results.append(paired.reshape((2 * LAYERS,) + paired.shape[2:]))
    return (input_gradient, results[0], results[1], results[2])
```

```python
import functools
import jax
import jax.numpy as jnp
from jax import lax
from jax.experimental import pallas as pl
from jax.experimental.pallas import tpu as pltpu
from jax.sharding import PartitionSpec as P

epsilon = 1e-05
momentum_decay = 0.9


def passed_along(block, axis, distance):
    devices = range(lax.axis_size(axis))
    route = [(i - distance, i) for i in devices if i - distance in devices]
    return lax.ppermute(block, axis, route)


def partner(block, axis, distance):
    count = lax.axis_size(axis)
    route = []
    for low in range(count):
        high = low | 1 << distance
        if high != low and high < count:
            route += [(low, high), (high, low)]
    return lax.ppermute(block, axis, route)


def contract_last(left, right):
    return lax.dot_general(
        left, right, (((1,), (1,)), ((), ())), preferred_element_type=jnp.float32
    )


def contract_rows(left, right):
    return lax.dot_general(
        left, right, (((0,), (0,)), ((), ())), preferred_element_type=jnp.float32
    )


def rounded(values):
    return lax.optimization_barrier(values.astype(jnp.bfloat16)).astype(jnp.float32)


def project(rows, gate_w, up_w):
    gate = jnp.dot(rows, gate_w, preferred_element_type=jnp.float32)
    up = jnp.dot(rows, up_w, preferred_element_type=jnp.float32)
    return (gate, up)


def backward_factors(incoming_rows, gate, up, down_w):
    hidden_grad = contract_last(incoming_rows, down_w)
    sigma = jax.nn.sigmoid(gate)
    silu = gate * sigma
    hidden = (silu * up).astype(jnp.bfloat16)
    gate_grad = (hidden_grad * up * sigma * (1.0 + gate * (1.0 - sigma))).astype(jnp.bfloat16)
    up_grad = (hidden_grad * silu).astype(jnp.bfloat16)
    return (hidden, gate_grad, up_grad)


def owned(array, start, size, axis):
    return lax.dynamic_slice_in_dim(array, start, size, axis)


def shards(
    layer_inputs,
    cotangent,
    gate_weight,
    up_weight,
    down_weight,
    gate_momentum,
    up_momentum,
    down_momentum,
):
    segments = lax.axis_size("segment")
    depth = segments // 2
    segment = lax.axis_index("segment")
    direction = segment % 2
    lower = direction == 0
    position = segment // 2
    gate_w = gate_weight[0]
    up_w = up_weight[0]
    down_w = down_weight[0]
    inputs = layer_inputs[0].astype(jnp.float32)
    micro, rows_dev, width = inputs.shape
    half = width // 2
    hidden_dev = gate_w.shape[1]
    total_rows = rows_dev * lax.axis_size("tp")
    inverse_norm = lax.rsqrt(jnp.mean(inputs * inputs, axis=-1, keepdims=True) + epsilon)
    exact = inputs * inverse_norm
    normed = exact.astype(jnp.bfloat16)
    entry = lax.dynamic_index_in_dim(cotangent, direction, 0, keepdims=False)
    ticks = depth + micro - 1
    wide_store = jnp.zeros((micro, total_rows, width), jnp.bfloat16)
    narrow_store = jnp.zeros((micro, total_rows, hidden_dev), jnp.bfloat16)
    extra = (wide_store, narrow_store, narrow_store, narrow_store) + (wide_store,)

    def process(tick, received, state):
        outgoing, backs, extra = state
        index = tick - position
        active = (index >= 0) & (index < micro)
        slot = jnp.clip(index, 0, micro - 1)
        local_in = jnp.where(position == 0, entry[slot], received)
        incoming_rows = lax.all_gather(local_in, "tp", axis=0, tiled=True)
        full_rows = lax.all_gather(normed[slot], "tp", axis=0, tiled=True)

        def factors():
            gate, up = project(full_rows, gate_w, up_w)
            return backward_factors(incoming_rows, gate, up, down_w)

        def resting():
            blank = jnp.zeros((total_rows, hidden_dev), jnp.bfloat16)
            return (blank, blank, blank)

        hidden, gate_grad, up_grad = lax.cond(active, factors, resting)
        count = lax.axis_size("tp") * rows_dev

        def compute():
            return contract_last(gate_grad, gate_w) + contract_last(up_grad, up_w)

        def quiet():
            return jnp.zeros((count, width), jnp.float32)

        normed_grad = lax.psum_scatter(
            lax.cond(active, compute, quiet).astype(jnp.bfloat16),
            "tp",
            scatter_dimension=0,
            tiled=True,
        ).astype(jnp.float32)
        scale = inverse_norm[slot]
        base = exact[slot]
        back = local_in.astype(jnp.float32) + scale * (
            normed_grad - base * jnp.mean(normed_grad * base, axis=-1, keepdims=True)
        )
        back = back.astype(jnp.bfloat16)
        backs = lax.dynamic_update_index_in_dim(
            backs, jnp.where(active, back, backs[slot]), slot, 0
        )
        fresh = (incoming_rows, hidden, gate_grad, up_grad) + (full_rows,)
        extra = tuple(
            (
                lax.dynamic_update_index_in_dim(
                    store, jnp.where(active, item, store[slot]), slot, 0
                )
                for store, item in zip(extra, fresh)
            )
        )
        return (back, backs, extra)

    zero_rows = jnp.zeros((rows_dev, width), jnp.bfloat16)
    state = process(
        0, zero_rows, (zero_rows, jnp.zeros((micro, rows_dev, width), jnp.bfloat16), extra)
    )

    def advance(tick, state):
        received = passed_along(state[0], "segment", 2)
        return process(tick, received, state)

    outgoing, backs, extra = lax.fori_loop(1, ticks, advance, state)
    keep_start = jnp.where(lower, 0, half)
    send_start = half - keep_start
    flat_rows = micro * total_rows
    normed_all = extra[4]
    normed_flat = normed_all.reshape(flat_rows, width)
    incoming_flat = extra[0].reshape(flat_rows, width)
    hidden_flat = extra[1].reshape(flat_rows, hidden_dev)
    gate_flat = extra[2].reshape(flat_rows, hidden_dev)
    up_flat = extra[3].reshape(flat_rows, hidden_dev)
    arrived = partner(
        (
            owned(normed_flat, send_start, half, 1),
            owned(incoming_flat, send_start, half, 1),
            hidden_flat,
            gate_flat,
            up_flat,
        ),
        "segment",
        0,
    )
    normed_keep = owned(normed_flat, keep_start, half, 1)
    incoming_keep = owned(incoming_flat, keep_start, half, 1)
    gate_share = contract_rows(normed_keep, gate_flat) + rounded(
        contract_rows(arrived[0], arrived[3])
    )
    up_share = contract_rows(normed_keep, up_flat) + rounded(contract_rows(arrived[0], arrived[4]))
    down_share = contract_rows(hidden_flat, incoming_keep) + rounded(
        contract_rows(arrived[2], arrived[1])
    )
    new_gate = (momentum_decay * gate_momentum[0] + gate_share)[None]
    new_up = (momentum_decay * up_momentum[0] + up_share)[None]
    new_down = (momentum_decay * down_momentum[0] + down_share)[None]
    return (backs[None], new_gate, new_up, new_down)


CHUNKS = 4
VMEM_LIMIT = 42 << 20
ORDER = (
    ("R00 R01 R02 R03", "F00 F01 K00 F02", "K01 F03 K02 K03"),
    ("E0 P00 S0 P01", "P02 Q00 n1 P03", "Q01 Q02 Q03"),
    ("h10 h11 h12 h13", "N1 R10 R11", "R12 R13"),
    ("G00 G01 G02 G03", "f10 f11 K10 f12", "K11 f13 K12 K13", "E1"),
    ("P10 S1 P11 P12", "Q10 P13 Q11", "Q12 Q13"),
    ("X00 X01 X02 X03", "L0 U0 G10 X10", "G11 X11 G12 X12", "G13 X13"),
    ("V0 l0 u0", "L1 l1"),
)


def scope(name):
    return jax.named_scope(name)


def update(d, k, nrm, inc, hidden, gate_g, up_g, accs, news, scale=False, done=None):
    _, chunks, sides, n, rows, span = nrm.shape
    total = sides * n * rows
    hid = hidden.shape[2]
    keep = d * (chunks // 2)
    step = 256

    def add(which, where, value):
        old = accs[which][where]
        news[which][where] = (old * momentum_decay if scale else old) + value
        if done is not None:
            done(which, where)

    @pl.loop(0, chunks // 2)
    def _(j):
        place = pl.ds(pl.multiple_of(j * span, span), span)
        lhs = nrm[k, keep + j].reshape(total, span)
        rhs = inc[k, keep + j].reshape(total, span)

        @pl.loop(0, hid // step)
        def _(i):
            piece = pl.ds(pl.multiple_of(i * step, step), step)
            add(0, (place, piece), contract_rows(lhs, gate_g[k, :, piece]))
            add(1, (place, piece), contract_rows(lhs, up_g[k, :, piece]))
            add(2, (piece, place), contract_rows(hidden[k, :, piece], rhs))


def apply_kernel(
    back, gate_acc, up_acc, down_acc, nrm, inc, hidden, gate_g, up_g,
    back_out, gate_out, up_out, down_out, gate_new, up_new, down_new, sems,
):
    d = lax.rem(lax.axis_index("segment"), 2)
    accs = (gate_acc, up_acc, down_acc)
    news = (gate_new, up_new, down_new)
    outs = (gate_out, up_out, down_out)
    backs = pltpu.make_async_copy(back, back_out, sems.at[3])
    backs.start()

    def done(which, where):
        pltpu.make_async_copy(
            news[which].at[where], outs[which].at[where], sems.at[which]
        ).start()

    update(d, nrm.shape[0] - 1, nrm, inc, hidden, gate_g, up_g, accs, news, done=done)
    for which in range(3):
        pltpu.make_async_copy(news[which], outs[which], sems.at[which]).wait()
    backs.wait()


def semaphore_keys(micro, chunks, n):
    slots = [1] + list(range(2, n, 2))
    bits = n.bit_length() - 1
    keys = []
    for k in range(micro):
        keys += [("normed", k, m) for m in slots]
        keys += [("mirror", k), ("pass", k)]
        keys += [("sum", k, chunks, b) for b in range(bits)]
        for c in range(chunks):
            keys += [("rows", k, c, m) for m in slots]
            keys += [("sum", k, c, b) for b in range(bits)]
            keys += [("mirror", k, c), ("pass", k, c), ("hop", k, c)]
    return {key: i for i, key in enumerate(keys)}


def relay_kernel(
    n,
    depth,
    li_hbm,
    cot_hbm,
    gate_hbm,
    up_hbm,
    down_hbm,
    gate_m,
    up_m,
    down_m,
    back_ref,
    gate_acc,
    up_acc,
    down_acc,
    nrm,
    inc,
    hidden,
    gate_g,
    up_g,
    gate_w,
    up_w,
    down_w,
    gate_t,
    up_t,
    down_t,
    li_ref,
    cot_ref,
    slope,
    silu_s,
    slant,
    grad_s,
    exact_s,
    inv_s,
    mean_s,
    parts,
    rs_recv,
    stats,
    st_recv,
    z_send,
    load_sem,
    cot_sem,
    ssem,
    rsem,
):
    micro, rows, width = li_ref.shape
    hid = down_w.shape[0]
    chunks, span = nrm.shape[1], nrm.shape[5]
    total = n * rows
    half = width // 2
    bits = n.bit_length() - 1
    s = lax.axis_index("segment")
    t = lax.axis_index("tp")
    p = lax.div(s, 2)
    d = lax.rem(s, 2)
    mirror = s + 1 - 2 * d
    first = p == 0
    early = jnp.logical_and(p > 0, p * 2 >= depth)
    last = p == depth - 1

    def flip(mask):
        value = t
        for b in range(bits):
            if mask >> b & 1:
                value = value + (1 << b) * (1 - 2 * lax.rem(lax.div(t, 1 << b), 2))
        return value

    def cols(c):
        return pl.ds(c * span, span)

    barrier = pltpu.get_barrier_semaphore()

    def greet(device):
        pl.semaphore_signal(
            barrier, inc=1, device_id=device, device_id_type=pl.DeviceIdType.MESH
        )

    for b in range(bits):
        greet({"tp": flip(1 << b)})
    greet({"segment": mirror})

    @pl.when(p > 0)
    def _():
        greet({"segment": s - 2})

    @pl.when(p < depth - 1)
    def _():
        greet({"segment": s + 2})

    sources = (li_hbm, down_hbm, gate_hbm, up_hbm, gate_m, up_m, down_m)
    targets = (li_ref, down_w, gate_w, up_w, gate_acc, up_acc, down_acc)
    loads = [
        pltpu.make_async_copy(a, b, load_sem.at[i])
        for i, (a, b) in enumerate(zip(sources, targets))
    ]

    cot_load = pltpu.make_async_copy(cot_hbm.at[d], cot_ref, cot_sem)
    loads[0].start()
    pl.when(first)(cot_load.start)
    for load in loads[1:4]:
        load.start()

    keys = semaphore_keys(micro, chunks, n)

    def copy(group, key, src, dst, device):
        return pltpu.make_async_remote_copy(
            src_ref=src,
            dst_ref=dst,
            send_sem=ssem.at[group],
            recv_sem=rsem.at[keys[key]],
            device_id=device,
            device_id_type=pl.DeviceIdType.MESH,
        )

    def arrived(key, ref):
        copy(0, key, ref, ref, {"tp": flip(1)}).wait_recv()

    evens = sorted(range(2, n, 2), key=lambda m: -(m & -m))

    def spread(ref, key, m, b):
        block = ref.at[flip(m)]
        slot = m | 1 << b
        copy(0, key + (slot if b else 1,), block, block, {"tp": flip(1 << b)}).start()

    def cross(kind, k, c, m, start=True):
        if kind:
            source, target, key = inc.at[k, c, 0], inc.at[k, c, 1], ("mirror", k, c)
            source, target = source.at[flip(m)], target.at[flip(m)]
        else:
            source, target, key = nrm.at[k, :, 0, flip(m)], nrm.at[k, :, 1, flip(m)], ("mirror", k)
        copy(2, key, source, target, {"segment": mirror}).start()

    def normed_copy(k, m, b):
        block = nrm.at[k, :, 0, flip(m)]
        copy(0, ("normed", k, m | 1 << b if b else 1), block, block, {"tp": flip(1 << b)}).start()

    def normed_start(k):
        for b in reversed(range(bits)):
            normed_copy(k, 0, b)

    def normed_forward(k):
        for m in evens:
            arrived(("normed", k, m), nrm.at[k, :, 0, flip(m)])
            for b in reversed(range(bits)):
                if 1 << b < (m & -m):
                    normed_copy(k, m, b)
            cross(0, k, 0, m)

    def normed_wait(k):
        arrived(("normed", k, 1), nrm.at[k, :, 0, pl.ds(0, n // 2)])

    def rows_start(k, c):
        for b in reversed(range(bits)):
            spread(inc.at[k, c, 0], ("rows", k, c), 0, b)

    def rows_forward(k, c):
        for m in evens:
            arrived(("rows", k, c, m), inc.at[k, c, 0, flip(m)])
            for b in reversed(range(bits)):
                if 1 << b < (m & -m):
                    spread(inc.at[k, c, 0], ("rows", k, c), m, b)
            cross(1, k, c, m)

    def rows_wait(k, c):
        arrived(("rows", k, c, 1), inc.at[k, c, 0, pl.ds(0, n // 2)])

    def normed_pass(k):
        arrived(("mirror", k), nrm.at[k, :, 1, pl.ds(0, n // 2)])
        for m in range(0, n, 2):
            block = nrm.at[k, :, 1, flip(m)]
            copy(2, ("pass", k), block, block, {"tp": flip(1)}).start()

    def rows_pass(k, c):
        arrived(("mirror", k, c), inc.at[k, c, 1, pl.ds(0, n // 2)])
        for m in range(0, n, 2):
            block = inc.at[k, c, 1, flip(m)]
            copy(2, ("pass", k, c), block, block, {"tp": flip(1)}).start()

    def turn(source, target):
        step = 256

        @pl.loop(0, source.shape[1] // step)
        def _(j):
            piece = pl.ds(pl.multiple_of(j * step, step), step)
            target[piece, :] = source[:, piece].T

    def forward(side, k):
        step = min(256, hid)
        here = pl.ds(side * total, total)

        @pl.loop(0, hid // step)
        def _(j):
            piece = pl.ds(pl.multiple_of(j * step, step), step)
            g = jnp.zeros((total, step), jnp.float32)
            u = jnp.zeros((total, step), jnp.float32)
            for c in range(chunks):
                lhs = nrm[k, c, side].reshape(total, span)
                g = g + jnp.dot(lhs, gate_w[cols(c), piece], preferred_element_type=jnp.float32)
                u = u + jnp.dot(lhs, up_w[cols(c), piece], preferred_element_type=jnp.float32)
            sigma = jax.nn.sigmoid(g)
            sl = g * sigma
            sp = u * sigma * (1.0 + g * (1.0 - sigma))
            hidden[k, here, piece] = (sl * u).astype(jnp.bfloat16)
            slope[k, here, piece] = sp
            silu_s[k, here, piece] = sl
            if side == 0:
                slant[k, :, piece] = sp * g + sl * u

    def accumulate(side, k, c):
        lhs = inc[k, c, side].reshape(total, span)
        value = jnp.dot(lhs, down_t[cols(c), :], preferred_element_type=jnp.float32)
        if c:
            value = grad_s[side] + value
        grad_s[side] = value

    def factors(side, k):
        here = pl.ds(side * total, total)
        step = min(128, hid)
        sums = jnp.zeros((total, step), jnp.float32)
        for j in range(hid // step):
            piece = pl.ds(j * step, step)
            grad = grad_s[side, :, piece]
            gate_g[k, here, piece] = (grad * slope[k, here, piece]).astype(jnp.bfloat16)
            up_g[k, here, piece] = (grad * silu_s[k, here, piece]).astype(jnp.bfloat16)
            if side == 0:
                sums = sums + grad * slant[k, :, piece]
        if side == 0:
            stats[k] = sums.reshape(n, rows, step)

    def partial_grads(k, c):
        gg = gate_g[k, :total, :]
        ug = up_g[k, :total, :]
        part = jnp.dot(gg, gate_t[:, cols(c)], preferred_element_type=jnp.float32)
        part = part + jnp.dot(ug, up_t[:, cols(c)], preferred_element_type=jnp.float32)
        parts[k, c] = part.astype(jnp.bfloat16).reshape(n, rows, span)

    def rs_refs(k, c):
        if c == chunks:
            return stats.at[k], st_recv.at[k]
        return parts.at[k, c], rs_recv.at[k, c]

    def rs_round(k, c, b):
        source, target = rs_refs(k, c)
        for m in range(0, n, 1 << (b + 1)):
            q = m | 1 << b
            if b:
                value = source[flip(q)].astype(jnp.float32)
                for lower in range(b):
                    value = value + target[q | 1 << lower].astype(jnp.float32)
                source[flip(q)] = value.astype(source.dtype)
            copy(
                1 if c == chunks else 0,
                ("sum", k, c, b),
                source.at[flip(q)],
                target.at[q],
                {"tp": flip(1 << b)},
            ).start()

    def rs_wait(k, c, b):
        arrived(("sum", k, c, b), rs_refs(k, c)[1].at[pl.ds(0, n >> (b + 1))])

    def rs_total(k, c):
        source, target = rs_refs(k, c)
        value = source[t].astype(jnp.float32)
        for b in range(bits):
            value = value + target[1 << b].astype(jnp.float32)
        return value

    def receive(k, c):
        @pl.when(jnp.logical_not(first))
        def _():
            arrived(("hop", k, c), inc.at[k, c, 0, t])
            rows_start(k, c)
            cross(1, k, c, 0)

    def reduce(k, c):
        for b in range(1, bits):
            rs_wait(k, c, b - 1)
            rs_round(k, c, b)

    def finish(k, c):
        if c == 0:
            rs_wait(k, chunks, bits - 1)
            sums = rs_total(k, chunks)
            mean_s[k] = jnp.sum(sums, axis=-1, keepdims=True) * (1.0 / width)
        rs_wait(k, c, bits - 1)
        value = rs_total(k, c)
        own = inc[k, c, 0, t].astype(jnp.float32)
        back = own + inv_s[k] * (value - exact_s[k, c] * mean_s[k])
        back = back.astype(jnp.bfloat16)
        z_send[k, c] = back

        @pl.when(p < depth - 1)
        def _():
            target = inc.at[k, c, 0, t]
            copy(3, ("hop", k, c), z_send.at[k, c], target, {"segment": s + 2}).start()

        back_ref[k, :, cols(c)] = back

    loads[0].wait()
    for k in range(micro):
        x = li_ref[k].astype(jnp.float32)
        inv = lax.rsqrt(jnp.mean(x * x, axis=-1, keepdims=True) + epsilon)
        inv_s[k] = inv
        for c in range(chunks):
            exact = x[:, c * span : (c + 1) * span] * inv
            exact_s[k, c] = exact
            nrm[k, c, 0, t] = exact.astype(jnp.bfloat16)

    @pl.when(first)
    def _():
        cot_load.wait()
        for k in range(micro):
            for c in range(chunks):
                inc[k, c, 0, t] = cot_ref[k, :, cols(c)]

    peers = bits + 1 + jnp.minimum(p, 1) + jnp.minimum(depth - 1 - p, 1)
    with scope("barrier"):
        pl.semaphore_wait(barrier, peers)

    normed_start(0)
    for k in range(micro):
        cross(0, k, 0, 0)

    def mirror_forward():
        for k in range(micro):
            normed_pass(k)
        for k in range(micro):
            arrived(("pass", k), nrm.at[k, :, 1, pl.ds(0, n // 2)])
            forward(1, k)

    def cot_start(k):
        @pl.when(first)
        def _():
            for c in range(chunks):
                rows_start(k, c)
            for c in range(chunks):
                cross(1, k, c, 0)

    with scope("t1"):
        loads[1].wait()
        turn(down_w, down_t)
    cot_start(0)
    with scope("t2"):
        loads[2].wait()
        loads[3].wait()
        for load in loads[4:]:
            load.start()
        turn(gate_w, gate_t)
    for k in range(1, micro):
        normed_start(k)
    with scope("nf0"):
        pl.when(jnp.logical_not(first))(lambda: normed_forward(0))
    with scope("t3"):
        turn(up_w, up_t)
    for k in range(1, micro):
        cot_start(k)
    with scope("nf0f"):
        pl.when(first)(lambda: normed_forward(0))
    with scope("nw0"):
        normed_wait(0)
    with scope("fw0"):
        forward(0, 0)

    def later():
        for k in range(1, micro):
            normed_forward(k)
            normed_wait(k)
            forward(0, k)

    with scope("fw1"):
        pl.when(jnp.logical_not(first))(later)
    with scope("mf"):
        pl.when(early)(mirror_forward)

    def op_R(k, c):
        receive(k, c)

    def op_F(k, c):
        rows_forward(k, c)

    def op_f(k, c):
        pl.when(jnp.logical_not(first))(lambda: rows_forward(k, c))

    def op_h(k, c):
        pl.when(first)(lambda: rows_forward(k, c))

    def op_n(k):
        pl.when(first)(lambda: normed_forward(k))

    def op_N(k):
        def run():
            normed_wait(k)
            forward(0, k)

        pl.when(first)(run)

    def op_K(k, c):
        rows_wait(k, c)
        accumulate(0, k, c)

    def op_E(k):
        factors(0, k)
        rs_round(k, chunks, 0)

    def op_P(k, c):
        partial_grads(k, c)
        rs_round(k, c, 0)

    def op_S(k):
        reduce(k, chunks)

    def op_Q(k, c):
        reduce(k, c)

    def op_G(k, c):
        finish(k, c)

    def op_X(k, c):
        rows_pass(k, c)

    def op_M(k):
        for c in range(chunks):
            arrived(("pass", k, c), inc.at[k, c, 1, pl.ds(0, n // 2)])
            accumulate(1, k, c)
        factors(1, k)

    def op_A(k):
        if k == 0:
            for load in loads[4:]:
                load.wait()
        accs = (gate_acc, up_acc, down_acc)
        update(d, k, nrm, inc, hidden, gate_g, up_g, accs, accs, scale=k == 0)

    def op_L(k):
        pl.when(early)(lambda: op_M(k))

    def op_U(k):
        pl.when(last)(lambda: op_A(k))

    def op_V(k):
        pl.when(jnp.logical_not(early))(mirror_forward)

    def op_l(k):
        pl.when(jnp.logical_not(early))(lambda: op_M(k))

    def op_u(k):
        pl.when(jnp.logical_not(last))(lambda: op_A(k))

    ops = dict(
        R=op_R, F=op_F, f=op_f, h=op_h, N=op_N, n=op_n, K=op_K, E=op_E, P=op_P, S=op_S,
        Q=op_Q, G=op_G, X=op_X, M=op_M, A=op_A, L=op_L, U=op_U, V=op_V, l=op_l, u=op_u,
    )
    for name in [x for line in ORDER for part in line for x in part.split()]:
        with scope(name):
            ops[name[0]](*(int(x) for x in name[1:]))

    block = rows * span
    sizes = (
        micro * chunks * (n - 1) * 3 * block,
        micro * (n - 1) * rows * 128,
        micro * chunks * 2 * n * block,
        micro * chunks * block,
    )

    def sends_done(group, ref):
        view = ref.at[pl.ds(0, sizes[group] // ref.shape[1])]
        copy(group, ("normed", 0, 1), view, view, {"tp": flip(1)}).wait_send()

    with scope("sends"):
        sends_done(0, gate_w)
        sends_done(1, gate_acc)
        sends_done(2, gate_w)
        pl.when(p < depth - 1)(lambda: sends_done(3, gate_w))


def relayed(
    segments,
    n,
    layer_inputs,
    cotangent,
    gate_weight,
    up_weight,
    down_weight,
    gate_momentum,
    up_momentum,
    down_momentum,
):
    _, micro, rows, width = layer_inputs.shape
    hid = gate_weight.shape[2]
    half = width // 2
    chunks = CHUNKS
    span = width // chunks
    total = n * rows
    hbm = pl.BlockSpec(memory_space=pl.ANY)
    bf, f32 = jnp.bfloat16, jnp.float32
    ends = pl.pallas_call(
        functools.partial(relay_kernel, n, segments // 2),
        name="relay",
        out_shape=(
            pltpu.VMEM((micro, rows, width), bf),
            pltpu.VMEM((half, hid), f32),
            pltpu.VMEM((half, hid), f32),
            pltpu.VMEM((hid, half), f32),
            pltpu.VMEM((micro, chunks, 2, n, rows, span), bf),
            pltpu.VMEM((micro, chunks, 2, n, rows, span), bf),
            pltpu.VMEM((micro, 2 * total, hid), bf),
            pltpu.VMEM((micro, 2 * total, hid), bf),
            pltpu.VMEM((micro, 2 * total, hid), bf),
        ),
        in_specs=[hbm] * 8,
        scratch_shapes=[
            pltpu.VMEM((width, hid), bf),
            pltpu.VMEM((width, hid), bf),
            pltpu.VMEM((hid, width), bf),
            pltpu.VMEM((hid, width), bf),
            pltpu.VMEM((hid, width), bf),
            pltpu.VMEM((width, hid), bf),
            pltpu.VMEM((micro, rows, width), bf),
            pltpu.VMEM((micro, rows, width), bf),
            pltpu.VMEM((micro, 2 * total, hid), f32),
            pltpu.VMEM((micro, 2 * total, hid), f32),
            pltpu.VMEM((micro, total, hid), f32),
            pltpu.VMEM((2, total, hid), f32),
            pltpu.VMEM((micro, chunks, rows, span), f32),
            pltpu.VMEM((micro, rows, 1), f32),
            pltpu.VMEM((micro, rows, 1), f32),
            pltpu.VMEM((micro, chunks, n, rows, span), bf),
            pltpu.VMEM((micro, chunks, n, rows, span), bf),
            pltpu.VMEM((micro, n, rows, 128), f32),
            pltpu.VMEM((micro, n, rows, 128), f32),
            pltpu.VMEM((micro, chunks, rows, span), bf),
            pltpu.SemaphoreType.DMA((7,)),
            pltpu.SemaphoreType.DMA(()),
            pltpu.SemaphoreType.DMA((4,)),
            pltpu.SemaphoreType.DMA((len(semaphore_keys(micro, chunks, n)),)),
        ],
        compiler_params=pltpu.CompilerParams(
            collective_id=0, has_side_effects=True, vmem_limit_bytes=VMEM_LIMIT
        ),
    )(
        layer_inputs[0],
        cotangent,
        gate_weight[0],
        up_weight[0],
        down_weight[0],
        gate_momentum[0],
        up_momentum[0],
        down_momentum[0],
    )
    vmem = pl.BlockSpec(memory_space=pltpu.VMEM)
    back, new_gate, new_up, new_down = pl.pallas_call(
        apply_kernel,
        name="apply",
        out_shape=(
            jax.ShapeDtypeStruct((micro, rows, width), bf),
            jax.ShapeDtypeStruct((half, hid), f32),
            jax.ShapeDtypeStruct((half, hid), f32),
            jax.ShapeDtypeStruct((hid, half), f32),
        ),
        in_specs=[vmem] * 9,
        out_specs=(hbm,) * 4,
        scratch_shapes=[
            pltpu.VMEM((half, hid), f32),
            pltpu.VMEM((half, hid), f32),
            pltpu.VMEM((hid, half), f32),
            pltpu.SemaphoreType.DMA((4,)),
        ],
        compiler_params=pltpu.CompilerParams(vmem_limit_bytes=13 << 20),
    )(*ends)
    return (back[None], new_gate[None], new_up[None], new_down[None])


def choose(segments, n, *arrays):
    rows = arrays[0].shape[2]
    if rows % 16 == 0 and n > 1 and n & (n - 1) == 0 and segments > 2:
        return relayed(segments, n, *arrays)
    return shards(*arrays)


def solution(mesh):
    body = functools.partial(choose, mesh.shape["segment"], mesh.shape["tp"])
    return jax.shard_map(
        body,
        mesh=mesh,
        in_specs=(
            P("segment", None, "tp", None),
            P(None, None, "tp", None),
            P("segment", None, "tp"),
            P("segment", None, "tp"),
            P("segment", "tp", None),
            P("segment", None, "tp"),
            P("segment", None, "tp"),
            P("segment", "tp", None),
        ),
        out_specs=(
            P("segment", None, "tp", None),
            P("segment", None, "tp"),
            P("segment", None, "tp"),
            P("segment", "tp", None),
        ),
        check_vma=False,
    )
```

```python
import functools
import jax
import jax.numpy as jnp
from jax import lax
from jax.experimental import pallas as pl
from jax.experimental.pallas import tpu as pltpu
from jax.sharding import PartitionSpec as P

epsilon = 1e-05
momentum_decay = 0.9


def passed_along(block, axis, distance):
    devices = range(lax.axis_size(axis))
    route = [(i - distance, i) for i in devices if i - distance in devices]
    return lax.ppermute(block, axis, route)


def partner(block, axis, distance):
    count = lax.axis_size(axis)
    route = []
    for low in range(count):
        high = low | 1 << distance
        if high != low and high < count:
            route += [(low, high), (high, low)]
    return lax.ppermute(block, axis, route)


def contract_last(left, right):
    return lax.dot_general(
        left, right, (((1,), (1,)), ((), ())), preferred_element_type=jnp.float32
    )


def contract_rows(left, right):
    return lax.dot_general(
        left, right, (((0,), (0,)), ((), ())), preferred_element_type=jnp.float32
    )


def rounded(values):
    return lax.optimization_barrier(values.astype(jnp.bfloat16)).astype(jnp.float32)


def project(rows, gate_w, up_w):
    gate = jnp.dot(rows, gate_w, preferred_element_type=jnp.float32)
    up = jnp.dot(rows, up_w, preferred_element_type=jnp.float32)
    return (gate, up)


def backward_factors(incoming_rows, gate, up, down_w):
    hidden_grad = contract_last(incoming_rows, down_w)
    sigma = jax.nn.sigmoid(gate)
    silu = gate * sigma
    hidden = (silu * up).astype(jnp.bfloat16)
    gate_grad = (hidden_grad * up * sigma * (1.0 + gate * (1.0 - sigma))).astype(jnp.bfloat16)
    up_grad = (hidden_grad * silu).astype(jnp.bfloat16)
    return (hidden, gate_grad, up_grad)


def owned(array, start, size, axis):
    return lax.dynamic_slice_in_dim(array, start, size, axis)


def shards(
    layer_inputs,
    cotangent,
    gate_weight,
    up_weight,
    down_weight,
    gate_momentum,
    up_momentum,
    down_momentum,
):
    segments = lax.axis_size("segment")
    depth = segments // 2
    segment = lax.axis_index("segment")
    direction = segment % 2
    lower = direction == 0
    position = segment // 2
    gate_w = gate_weight[0]
    up_w = up_weight[0]
    down_w = down_weight[0]
    inputs = layer_inputs[0].astype(jnp.float32)
    micro, rows_dev, width = inputs.shape
    half = width // 2
    hidden_dev = gate_w.shape[1]
    total_rows = rows_dev * lax.axis_size("tp")
    inverse_norm = lax.rsqrt(jnp.mean(inputs * inputs, axis=-1, keepdims=True) + epsilon)
    exact = inputs * inverse_norm
    normed = exact.astype(jnp.bfloat16)
    entry = lax.dynamic_index_in_dim(cotangent, direction, 0, keepdims=False)
    ticks = depth + micro - 1
    wide_store = jnp.zeros((micro, total_rows, width), jnp.bfloat16)
    narrow_store = jnp.zeros((micro, total_rows, hidden_dev), jnp.bfloat16)
    extra = (wide_store, narrow_store, narrow_store, narrow_store) + (wide_store,)

    def process(tick, received, state):
        outgoing, backs, extra = state
        index = tick - position
        active = (index >= 0) & (index < micro)
        slot = jnp.clip(index, 0, micro - 1)
        local_in = jnp.where(position == 0, entry[slot], received)
        incoming_rows = lax.all_gather(local_in, "tp", axis=0, tiled=True)
        full_rows = lax.all_gather(normed[slot], "tp", axis=0, tiled=True)

        def factors():
            gate, up = project(full_rows, gate_w, up_w)
            return backward_factors(incoming_rows, gate, up, down_w)

        def resting():
            blank = jnp.zeros((total_rows, hidden_dev), jnp.bfloat16)
            return (blank, blank, blank)

        hidden, gate_grad, up_grad = lax.cond(active, factors, resting)
        count = lax.axis_size("tp") * rows_dev

        def compute():
            return contract_last(gate_grad, gate_w) + contract_last(up_grad, up_w)

        def quiet():
            return jnp.zeros((count, width), jnp.float32)

        normed_grad = lax.psum_scatter(
            lax.cond(active, compute, quiet).astype(jnp.bfloat16),
            "tp",
            scatter_dimension=0,
            tiled=True,
        ).astype(jnp.float32)
        scale = inverse_norm[slot]
        base = exact[slot]
        back = local_in.astype(jnp.float32) + scale * (
            normed_grad - base * jnp.mean(normed_grad * base, axis=-1, keepdims=True)
        )
        back = back.astype(jnp.bfloat16)
        backs = lax.dynamic_update_index_in_dim(
            backs, jnp.where(active, back, backs[slot]), slot, 0
        )
        fresh = (incoming_rows, hidden, gate_grad, up_grad) + (full_rows,)
        extra = tuple(
            (
                lax.dynamic_update_index_in_dim(
                    store, jnp.where(active, item, store[slot]), slot, 0
                )
                for store, item in zip(extra, fresh)
            )
        )
        return (back, backs, extra)

    zero_rows = jnp.zeros((rows_dev, width), jnp.bfloat16)
    state = process(
        0, zero_rows, (zero_rows, jnp.zeros((micro, rows_dev, width), jnp.bfloat16), extra)
    )

    def advance(tick, state):
        received = passed_along(state[0], "segment", 2)
        return process(tick, received, state)

    outgoing, backs, extra = lax.fori_loop(1, ticks, advance, state)
    keep_start = jnp.where(lower, 0, half)
    send_start = half - keep_start
    flat_rows = micro * total_rows
    normed_all = extra[4]
    normed_flat = normed_all.reshape(flat_rows, width)
    incoming_flat = extra[0].reshape(flat_rows, width)
    hidden_flat = extra[1].reshape(flat_rows, hidden_dev)
    gate_flat = extra[2].reshape(flat_rows, hidden_dev)
    up_flat = extra[3].reshape(flat_rows, hidden_dev)
    arrived = partner(
        (
            owned(normed_flat, send_start, half, 1),
            owned(incoming_flat, send_start, half, 1),
            hidden_flat,
            gate_flat,
            up_flat,
        ),
        "segment",
        0,
    )
    normed_keep = owned(normed_flat, keep_start, half, 1)
    incoming_keep = owned(incoming_flat, keep_start, half, 1)
    gate_share = contract_rows(normed_keep, gate_flat) + rounded(
        contract_rows(arrived[0], arrived[3])
    )
    up_share = contract_rows(normed_keep, up_flat) + rounded(contract_rows(arrived[0], arrived[4]))
    down_share = contract_rows(hidden_flat, incoming_keep) + rounded(
        contract_rows(arrived[2], arrived[1])
    )
    new_gate = (momentum_decay * gate_momentum[0] + gate_share)[None]
    new_up = (momentum_decay * up_momentum[0] + up_share)[None]
    new_down = (momentum_decay * down_momentum[0] + down_share)[None]
    return (backs[None], new_gate, new_up, new_down)


CHUNKS = 4
VMEM_LIMIT = 42 << 20


def scope(name):
    return jax.named_scope(name)


def update(d, plan, nrm, inc, hidden, gate_g, up_g, flipped, accs, news, done=None):
    _, chunks, sides, n, rows, span = nrm.shape
    total = sides * n * rows
    hid = hidden.shape[2]
    keep = d * (chunks // 2)
    step = 256

    @pl.loop(0, chunks // 2)
    def _(j):
        place = pl.ds(pl.multiple_of(j * span, span), span)
        flipped[...] = nrm[plan[0][1][0], keep + j].reshape(total, span).T

        @pl.loop(0, hid // step)
        def _(i):
            piece = pl.ds(pl.multiple_of(i * step, step), step)
            for which, ks, scale in plan:
                where = (piece, place) if which == 2 else (place, piece)
                value = accs[which][where]
                if scale:
                    value = value * momentum_decay
                for k in ks:
                    if which == 2:
                        rhs = inc[k, keep + j].reshape(total, span)
                        value = value + contract_rows(hidden[k, :, piece], rhs)
                    else:
                        grads = (gate_g, up_g)[which][k, :, piece]
                        value = value + jnp.dot(
                            flipped[...], grads, preferred_element_type=jnp.float32
                        )
                news[which][where] = value
                if done is not None:
                    done(which, where)


def apply_kernel(
    back, gate_acc, up_acc, down_acc, nrm, inc, hidden, gate_g, up_g,
    back_out, gate_out, up_out, down_out, gate_new, up_new, down_new, flipped, sems,
):
    d = lax.rem(lax.axis_index("segment"), 2)
    accs = (gate_acc, up_acc, down_acc)
    news = (gate_new, up_new, down_new)
    outs = (gate_out, up_out, down_out)
    backs = pltpu.make_async_copy(back, back_out, sems.at[3])
    backs.start()

    def done(which, where):
        pltpu.make_async_copy(
            news[which].at[where], outs[which].at[where], sems.at[which]
        ).start()

    final = nrm.shape[0] - 1
    plan = ((0, (final,), False), (1, (final,), False), (2, range(final + 1), True))
    update(d, plan, nrm, inc, hidden, gate_g, up_g, flipped, accs, news, done=done)
    for which in range(3):
        pltpu.make_async_copy(news[which], outs[which], sems.at[which]).wait()
    backs.wait()


def semaphore_keys(micro, chunks, n):
    slots = [1] + list(range(2, n, 2))
    bits = n.bit_length() - 1
    keys = []
    for k in range(micro):
        keys += [("normed", k, m) for m in slots]
        keys += [("mirror", k), ("pass", k)]
        keys += [("sum", k, chunks, b) for b in range(bits)]
        for c in range(chunks):
            keys += [("rows", k, c, m) for m in slots]
            keys += [("sum", k, c, b) for b in range(bits)]
            keys += [("mirror", k, c), ("pass", k, c), ("hop", k, c)]
            keys += [("side", k, c)] if k else []
    return {key: i for i, key in enumerate(keys)}


def relay_kernel(
    n,
    depth,
    li_hbm,
    cot_hbm,
    gate_hbm,
    up_hbm,
    down_hbm,
    gate_m,
    up_m,
    down_m,
    back_ref,
    gate_acc,
    up_acc,
    down_acc,
    nrm,
    inc,
    hidden,
    gate_g,
    up_g,
    gate_w,
    up_w,
    down_w,
    gate_t,
    up_t,
    down_t,
    li_ref,
    cot_ref,
    slope,
    silu_s,
    slant,
    grad_s,
    exact_s,
    inv_s,
    mean_s,
    parts,
    rs_recv,
    stats,
    st_recv,
    z_send,
    z_side,
    flipped,
    load_sem,
    cot_sem,
    ssem,
    rsem,
):
    micro, rows, width = li_ref.shape
    hid = down_w.shape[0]
    chunks, span = nrm.shape[1], nrm.shape[5]
    total = n * rows
    half = width // 2
    bits = n.bit_length() - 1
    top = n // 2
    s = lax.axis_index("segment")
    t = lax.axis_index("tp")
    p = lax.div(s, 2)
    d = lax.rem(s, 2)
    mirror = s + 1 - 2 * d
    first = p == 0
    early = jnp.logical_and(p > 0, p * 2 >= depth)
    last = p == depth - 1

    def flip(mask):
        value = t
        for b in range(bits):
            if mask >> b & 1:
                value = value + (1 << b) * (1 - 2 * lax.rem(lax.div(t, 1 << b), 2))
        return value

    def cols(c):
        return pl.ds(c * span, span)

    barrier = pltpu.get_barrier_semaphore()

    def greet(device):
        pl.semaphore_signal(
            barrier, inc=1, device_id=device, device_id_type=pl.DeviceIdType.MESH
        )

    for b in range(bits):
        greet({"tp": flip(1 << b)})
    greet({"segment": mirror})

    @pl.when(p > 0)
    def _():
        greet({"segment": s - 2})

    @pl.when(p < depth - 1)
    def _():
        greet({"segment": s + 2})

    sources = (li_hbm, down_hbm, gate_hbm, up_hbm, gate_m, up_m, down_m)
    targets = (li_ref, down_w, gate_w, up_w, gate_acc, up_acc, down_acc)
    loads = [
        pltpu.make_async_copy(a, b, load_sem.at[i])
        for i, (a, b) in enumerate(zip(sources, targets))
    ]

    cot_load = pltpu.make_async_copy(cot_hbm.at[d], cot_ref, cot_sem)
    def start_weights():
        for load in loads[1:4]:
            load.start()

    loads[0].start()
    pl.when(first)(cot_load.start)
    pl.when(jnp.logical_not(first))(start_weights)

    keys = semaphore_keys(micro, chunks, n)

    def copy(group, key, src, dst, device):
        return pltpu.make_async_remote_copy(
            src_ref=src,
            dst_ref=dst,
            send_sem=ssem.at[group],
            recv_sem=rsem.at[keys[key]],
            device_id=device,
            device_id_type=pl.DeviceIdType.MESH,
        )

    def arrived(key, ref):
        copy(0, key, ref, ref, {"tp": flip(1)}).wait_recv()

    evens = sorted(range(2, n, 2), key=lambda m: -(m & -m))

    def spread(ref, key, m, b):
        block = ref.at[flip(m)]
        slot = m | 1 << b
        copy(0, key + (slot if b else 1,), block, block, {"tp": flip(1 << b)}).start()

    def cross(kind, k, c, m, start=True):
        if kind:
            source, target, key = inc.at[k, c, 0], inc.at[k, c, 1], ("mirror", k, c)
            source, target = source.at[flip(m)], target.at[flip(m)]
        else:
            source, target, key = nrm.at[k, :, 0, flip(m)], nrm.at[k, :, 1, flip(m)], ("mirror", k)
        copy(2, key, source, target, {"segment": mirror}).start()

    def normed_copy(k, m, b):
        block = nrm.at[k, :, 0, flip(m)]
        copy(0, ("normed", k, m | 1 << b if b else 1), block, block, {"tp": flip(1 << b)}).start()

    def normed_start(k):
        for b in reversed(range(bits)):
            normed_copy(k, 0, b)

    def normed_forward(k):
        for m in evens:
            arrived(("normed", k, m), nrm.at[k, :, 0, flip(m)])
            for b in reversed(range(bits)):
                if 1 << b < (m & -m):
                    normed_copy(k, m, b)
            cross(0, k, 0, m)

    def normed_wait(k):
        arrived(("normed", k, 1), nrm.at[k, :, 0, pl.ds(0, n // 2)])

    def rows_start(k, c):
        for b in reversed(range(bits)):
            spread(inc.at[k, c, 0], ("rows", k, c), 0, b)

    def rows_forward(k, c):
        for m in evens:
            arrived(("rows", k, c, m), inc.at[k, c, 0, flip(m)])
            for b in reversed(range(bits)):
                if 1 << b < (m & -m):
                    spread(inc.at[k, c, 0], ("rows", k, c), m, b)
            cross(1, k, c, m)

    def rows_wait(k, c):
        arrived(("rows", k, c, 1), inc.at[k, c, 0, pl.ds(0, n // 2)])

    def normed_pass(k):
        arrived(("mirror", k), nrm.at[k, :, 1, pl.ds(0, n // 2)])
        for m in range(0, n, 2):
            block = nrm.at[k, :, 1, flip(m)]
            copy(2, ("pass", k), block, block, {"tp": flip(1)}).start()

    def rows_pass(k, c):
        arrived(("mirror", k, c), inc.at[k, c, 1, pl.ds(0, n // 2)])
        for m in range(0, n, 2):
            block = inc.at[k, c, 1, flip(m)]
            copy(2, ("pass", k, c), block, block, {"tp": flip(1)}).start()

    def turn(source, target):
        step = 256

        @pl.loop(0, source.shape[1] // step)
        def _(j):
            piece = pl.ds(pl.multiple_of(j * step, step), step)
            target[piece, :] = source[:, piece].T

    def forward(side, k, also=False):
        step = min(256, hid)
        here = pl.ds(side * total, total)

        @pl.loop(0, hid // step)
        def _(j):
            piece = pl.ds(pl.multiple_of(j * step, step), step)
            g = jnp.zeros((total, step), jnp.float32)
            u = jnp.zeros((total, step), jnp.float32)
            for c in range(chunks):
                lhs = nrm[k, c, side].reshape(total, span)
                g = g + jnp.dot(lhs, gate_w[cols(c), piece], preferred_element_type=jnp.float32)
                u = u + jnp.dot(lhs, up_w[cols(c), piece], preferred_element_type=jnp.float32)
            sigma = jax.nn.sigmoid(g)
            sl = g * sigma
            sp = u * sigma * (1.0 + g * (1.0 - sigma))
            hidden[k, here, piece] = (sl * u).astype(jnp.bfloat16)
            slope[k, here, piece] = sp
            silu_s[k, here, piece] = sl
            if side == 0:
                slant[k, :, piece] = sp * g + sl * u
            if also:
                up_t[piece, :] = up_w[:, piece].T

    def accumulate(side, k, c):
        lhs = inc[k, c, side].reshape(total, span)
        value = jnp.dot(lhs, down_t[cols(c), :], preferred_element_type=jnp.float32)
        if c:
            value = grad_s[side] + value
        grad_s[side] = value

    def factors(side, k):
        here = pl.ds(side * total, total)
        step = min(128, hid)
        sums = jnp.zeros((total, step), jnp.float32)
        for j in range(hid // step):
            piece = pl.ds(j * step, step)
            grad = grad_s[side, :, piece]
            gate_g[k, here, piece] = (grad * slope[k, here, piece]).astype(jnp.bfloat16)
            up_g[k, here, piece] = (grad * silu_s[k, here, piece]).astype(jnp.bfloat16)
            if side == 0:
                sums = sums + grad * slant[k, :, piece]
        if side == 0:
            stats[k] = sums.reshape(n, rows, step)

    def partial_grads(k, c):
        gg = gate_g[k, :total, :]
        ug = up_g[k, :total, :]
        part = jnp.dot(gg, gate_t[:, cols(c)], preferred_element_type=jnp.float32)
        part = part + jnp.dot(ug, up_t[:, cols(c)], preferred_element_type=jnp.float32)
        parts[k, c] = part.astype(jnp.bfloat16).reshape(n, rows, span)

    def rs_refs(k, c):
        if c == chunks:
            return stats.at[k], st_recv.at[k]
        return parts.at[k, c], rs_recv.at[k, c]

    def rs_round(k, c, b):
        source, target = rs_refs(k, c)
        for m in range(0, n, 1 << (b + 1)):
            q = m | 1 << b
            if b:
                value = source[flip(q)].astype(jnp.float32)
                for lower in range(b):
                    value = value + target[q | 1 << lower].astype(jnp.float32)
                source[flip(q)] = value.astype(source.dtype)
            copy(
                1 if c == chunks else 0,
                ("sum", k, c, b),
                source.at[flip(q)],
                target.at[q],
                {"tp": flip(1 << b)},
            ).start()

    def rs_wait(k, c, b):
        arrived(("sum", k, c, b), rs_refs(k, c)[1].at[pl.ds(0, n >> (b + 1))])

    def rs_total(k, c):
        source, target = rs_refs(k, c)
        value = source[t].astype(jnp.float32)
        for b in range(bits):
            value = value + target[1 << b].astype(jnp.float32)
        return value

    def receive(k, c):
        arrived(("hop", k, c), inc.at[k, c, 0, t])
        if k == 0:
            rows_start(k, c)
        else:
            for b in range(bits - 1):
                spread(inc.at[k, c, 0], ("rows", k, c), 0, b)
        cross(1, k, c, 0)

    def detour(k, c):
        @pl.when(p < depth - 1)
        def _():
            arrived(("side", k, c), z_side.at[k - 1, c])
            target = inc.at[k, c, 0, flip(top)]
            device = {"segment": s + 2}
            copy(4, ("rows", k, c, top), z_side.at[k - 1, c], target, device).start()

    def reduce(k, c):
        for b in range(1, bits):
            rs_wait(k, c, b - 1)
            rs_round(k, c, b)

    def finish(k, c):
        if c == 0:
            rs_wait(k, chunks, bits - 1)
            sums = rs_total(k, chunks)
            mean_s[k] = jnp.sum(sums, axis=-1, keepdims=True) * (1.0 / width)
        rs_wait(k, c, bits - 1)
        value = rs_total(k, c)
        own = inc[k, c, 0, t].astype(jnp.float32)
        back = own + inv_s[k] * (value - exact_s[k, c] * mean_s[k])
        back = back.astype(jnp.bfloat16)
        z_send[k, c] = back

        @pl.when(p < depth - 1)
        def _():
            target = inc.at[k, c, 0, t]
            copy(3, ("hop", k, c), z_send.at[k, c], target, {"segment": s + 2}).start()
            if k:
                target = z_side.at[k - 1, c]
                copy(4, ("side", k, c), z_send.at[k, c], target, {"tp": flip(top)}).start()

        back_ref[k, :, cols(c)] = back

    loads[0].wait()

    @pl.when(first)
    def _():
        cot_load.wait()
        start_weights()

    for k in range(micro):
        x = li_ref[k].astype(jnp.float32)
        inv = lax.rsqrt(jnp.mean(x * x, axis=-1, keepdims=True) + epsilon)
        inv_s[k] = inv
        for c in range(chunks):
            exact = x[:, c * span : (c + 1) * span] * inv
            exact_s[k, c] = exact
            nrm[k, c, 0, t] = exact.astype(jnp.bfloat16)

    @pl.when(first)
    def _():
        for k in range(micro):
            for c in range(chunks):
                inc[k, c, 0, t] = cot_ref[k, :, cols(c)]

    peers = bits + 1 + jnp.minimum(p, 1) + jnp.minimum(depth - 1 - p, 1)
    with scope("barrier"):
        pl.semaphore_wait(barrier, peers)

    normed_start(0)
    for k in range(micro):
        cross(0, k, 0, 0)

    def mirror_forward():
        for k in range(micro):
            normed_pass(k)
        for k in range(micro):
            arrived(("pass", k), nrm.at[k, :, 1, pl.ds(0, n // 2)])
            forward(1, k)

    def cot_start(k):
        @pl.when(first)
        def _():
            for c in range(chunks):
                rows_start(k, c)
            for c in range(chunks):
                cross(1, k, c, 0)

    with scope("t1"):
        loads[1].wait()
        turn(down_w, down_t)
    cot_start(0)
    with scope("t2"):
        loads[2].wait()
        loads[3].wait()
        for load in loads[4:]:
            load.start()
        turn(gate_w, gate_t)
    for k in range(1, micro):
        normed_start(k)
    for k in range(1, micro):
        cot_start(k)
    with scope("nf0"):
        normed_forward(0)
    with scope("nw0"):
        normed_wait(0)
    with scope("fw0"):
        forward(0, 0, True)

    def project_all():
        for k in range(1, micro):
            normed_forward(k)
            normed_wait(k)
            forward(0, k)

    with scope("fw1"):
        pl.when(jnp.logical_not(first))(project_all)
    with scope("mf"):
        pl.when(early)(mirror_forward)

    def side_gather(k, c):
        arrived(("pass", k, c), inc.at[k, c, 1, pl.ds(0, n // 2)])
        accumulate(1, k, c)

    def gather(k, c):
        rows_wait(k, c)
        accumulate(0, k, c)

    def factor(k):
        factors(0, k)
        rs_round(k, chunks, 0)

    def partial(k, c):
        partial_grads(k, c)
        rs_round(k, c, 0)

    def change(k):
        if k == 0:
            for load in loads[4:]:
                load.wait()
        accs = (gate_acc, up_acc, down_acc)
        plan = ((0, (k,), k == 0), (1, (k,), k == 0))
        update(d, plan, nrm, inc, hidden, gate_g, up_g, flipped, accs, accs)

    def project(k):
        normed_wait(k)
        forward(0, k)

    def mirrored():
        pl.when(jnp.logical_not(early))(mirror_forward)

    def traced(name, step):
        return step

    R, F, K = traced("R", receive), traced("F", rows_forward), traced("K", gather)
    E, P = traced("E", factor), traced("P", partial)
    S, Q = traced("S", lambda k: reduce(k, chunks)), traced("Q", reduce)
    G, H, X = traced("G", finish), traced("H", detour), traced("X", rows_pass)
    N, W, V = traced("N", normed_forward), traced("W", project), traced("V", mirrored)
    m, M = traced("m", side_gather), traced("M", lambda k: factors(1, k))
    U = traced("U", change)

    def each(*pairs):
        for c in range(chunks):
            for step, k in pairs:
                step(k, c)

    def products(k, between=None, fill=None):
        for c in range(chunks):
            if c == 2:
                S(k)
            P(k, c)
            if c >= 2:
                Q(k, c - 2)
                if fill is not None:
                    fill(k - 1, c - 2)
        if between is not None:
            between(1)
        for c in range(chunks - 2, chunks):
            Q(k, c)
            if fill is not None:
                fill(k - 1, c)

    def finals():
        each((X, 0))
        each((G, 1))
        each((H, 1))
        each((X, 1))
        V()
        each((m, 0))
        M(0)
        U(0)
        each((m, 1))
        M(1)

    def play_first():
        each((F, 0))
        each((K, 0))
        E(0)
        products(0, between=N)
        each((F, 1))
        W(1)
        each((G, 0), (K, 1))
        E(1)
        products(1)
        finals()

    def play_middle():
        each((R, 0))
        each((F, 0))
        each((K, 0))
        E(0)
        products(0)
        each((R, 1))
        each((F, 1), (G, 0))
        each((K, 1))
        E(1)
        products(1)
        finals()

    def play_last():
        each((R, 0))
        each((F, 0))
        each((K, 0))
        E(0)
        products(0)
        each((R, 1))
        each((X, 0))
        each((F, 1))
        each((K, 1))
        E(1)
        products(1, fill=m)
        M(0)
        each((X, 1))
        each((G, 0))
        U(0)
        each((m, 1))
        M(1)
        each((G, 1))

    pl.when(first)(play_first)
    pl.when(jnp.logical_not(jnp.logical_or(first, last)))(play_middle)
    pl.when(last)(play_last)

    block = rows * span
    sizes = (
        micro * chunks * (n - 1) * 3 * block,
        micro * (n - 1) * rows * 128,
        micro * chunks * 2 * n * block,
        micro * chunks * block,
        2 * (micro - 1) * chunks * block,
        micro * chunks * (n - 1) * 3 * block - (micro - 1) * chunks * block,
    )

    def sends_done(group, ref, size=None):
        view = ref.at[pl.ds(0, sizes[group if size is None else size] // ref.shape[1])]
        copy(group, ("normed", 0, 1), view, view, {"tp": flip(1)}).wait_send()

    with scope("sends"):
        pl.when(first)(lambda: sends_done(0, gate_w))
        pl.when(jnp.logical_not(first))(lambda: sends_done(0, gate_w, 5))
        sends_done(1, gate_acc)
        sends_done(2, gate_w)

        @pl.when(p < depth - 1)
        def _():
            sends_done(3, gate_w)
            sends_done(4, gate_w)


def relayed(
    segments,
    n,
    layer_inputs,
    cotangent,
    gate_weight,
    up_weight,
    down_weight,
    gate_momentum,
    up_momentum,
    down_momentum,
):
    _, micro, rows, width = layer_inputs.shape
    hid = gate_weight.shape[2]
    half = width // 2
    chunks = CHUNKS
    span = width // chunks
    total = n * rows
    hbm = pl.BlockSpec(memory_space=pl.ANY)
    bf, f32 = jnp.bfloat16, jnp.float32
    ends = pl.pallas_call(
        functools.partial(relay_kernel, n, segments // 2),
        name="relay",
        out_shape=(
            pltpu.VMEM((micro, rows, width), bf),
            pltpu.VMEM((half, hid), f32),
            pltpu.VMEM((half, hid), f32),
            pltpu.VMEM((hid, half), f32),
            pltpu.VMEM((micro, chunks, 2, n, rows, span), bf),
            pltpu.VMEM((micro, chunks, 2, n, rows, span), bf),
            pltpu.VMEM((micro, 2 * total, hid), bf),
            pltpu.VMEM((micro, 2 * total, hid), bf),
            pltpu.VMEM((micro, 2 * total, hid), bf),
        ),
        in_specs=[hbm] * 8,
        scratch_shapes=[
            pltpu.VMEM((width, hid), bf),
            pltpu.VMEM((width, hid), bf),
            pltpu.VMEM((hid, width), bf),
            pltpu.VMEM((hid, width), bf),
            pltpu.VMEM((hid, width), bf),
            pltpu.VMEM((width, hid), bf),
            pltpu.VMEM((micro, rows, width), bf),
            pltpu.VMEM((micro, rows, width), bf),
            pltpu.VMEM((micro, 2 * total, hid), f32),
            pltpu.VMEM((micro, 2 * total, hid), f32),
            pltpu.VMEM((micro, total, hid), f32),
            pltpu.VMEM((2, total, hid), f32),
            pltpu.VMEM((micro, chunks, rows, span), f32),
            pltpu.VMEM((micro, rows, 1), f32),
            pltpu.VMEM((micro, rows, 1), f32),
            pltpu.VMEM((micro, chunks, n, rows, span), bf),
            pltpu.VMEM((micro, chunks, n, rows, span), bf),
            pltpu.VMEM((micro, n, rows, 128), f32),
            pltpu.VMEM((micro, n, rows, 128), f32),
            pltpu.VMEM((micro, chunks, rows, span), bf),
            pltpu.VMEM((micro - 1, chunks, rows, span), bf),
            pltpu.VMEM((span, 2 * total), bf),
            pltpu.SemaphoreType.DMA((7,)),
            pltpu.SemaphoreType.DMA(()),
            pltpu.SemaphoreType.DMA((5,)),
            pltpu.SemaphoreType.DMA((len(semaphore_keys(micro, chunks, n)),)),
        ],
        compiler_params=pltpu.CompilerParams(
            collective_id=0, has_side_effects=True, vmem_limit_bytes=VMEM_LIMIT
        ),
    )(
        layer_inputs[0],
        cotangent,
        gate_weight[0],
        up_weight[0],
        down_weight[0],
        gate_momentum[0],
        up_momentum[0],
        down_momentum[0],
    )
    vmem = pl.BlockSpec(memory_space=pltpu.VMEM)
    back, new_gate, new_up, new_down = pl.pallas_call(
        apply_kernel,
        name="apply",
        out_shape=(
            jax.ShapeDtypeStruct((micro, rows, width), bf),
            jax.ShapeDtypeStruct((half, hid), f32),
            jax.ShapeDtypeStruct((half, hid), f32),
            jax.ShapeDtypeStruct((hid, half), f32),
        ),
        in_specs=[vmem] * 9,
        out_specs=(hbm,) * 4,
        scratch_shapes=[
            pltpu.VMEM((half, hid), f32),
            pltpu.VMEM((half, hid), f32),
            pltpu.VMEM((hid, half), f32),
            pltpu.VMEM((span, 2 * total), bf),
            pltpu.SemaphoreType.DMA((4,)),
        ],
        compiler_params=pltpu.CompilerParams(vmem_limit_bytes=13 << 20),
    )(*ends)
    return (back[None], new_gate[None], new_up[None], new_down[None])


def choose(segments, n, *arrays):
    rows = arrays[0].shape[2]
    if rows % 16 == 0 and n == 4 and segments > 2 and arrays[0].shape[1] == 2:
        return relayed(segments, n, *arrays)
    return shards(*arrays)


def solution(mesh):
    body = functools.partial(choose, mesh.shape["segment"], mesh.shape["tp"])
    return jax.shard_map(
        body,
        mesh=mesh,
        in_specs=(
            P("segment", None, "tp", None),
            P(None, None, "tp", None),
            P("segment", None, "tp"),
            P("segment", None, "tp"),
            P("segment", "tp", None),
            P("segment", None, "tp"),
            P("segment", None, "tp"),
            P("segment", "tp", None),
        ),
        out_specs=(
            P("segment", None, "tp", None),
            P("segment", None, "tp"),
            P("segment", None, "tp"),
            P("segment", "tp", None),
        ),
        check_vma=False,
    )
```

```python
import functools
import jax
import jax.numpy as jnp
from jax import lax
from jax.experimental import pallas as pl
from jax.experimental.pallas import tpu as pltpu
from jax.sharding import PartitionSpec as P

epsilon = 1e-05
momentum_decay = 0.9


def passed_along(block, axis, distance):
    devices = range(lax.axis_size(axis))
    route = [(i - distance, i) for i in devices if i - distance in devices]
    return lax.ppermute(block, axis, route)


def partner(block, axis, distance):
    count = lax.axis_size(axis)
    route = []
    for low in range(count):
        high = low | 1 << distance
        if high != low and high < count:
            route += [(low, high), (high, low)]
    return lax.ppermute(block, axis, route)


def contract_last(left, right):
    return lax.dot_general(
        left, right, (((1,), (1,)), ((), ())), preferred_element_type=jnp.float32
    )


def contract_rows(left, right):
    return lax.dot_general(
        left, right, (((0,), (0,)), ((), ())), preferred_element_type=jnp.float32
    )


def rounded(values):
    return lax.optimization_barrier(values.astype(jnp.bfloat16)).astype(jnp.float32)


def project(rows, gate_w, up_w):
    gate = jnp.dot(rows, gate_w, preferred_element_type=jnp.float32)
    up = jnp.dot(rows, up_w, preferred_element_type=jnp.float32)
    return (gate, up)


def backward_factors(incoming_rows, gate, up, down_w):
    hidden_grad = contract_last(incoming_rows, down_w)
    sigma = jax.nn.sigmoid(gate)
    silu = gate * sigma
    hidden = (silu * up).astype(jnp.bfloat16)
    gate_grad = (hidden_grad * up * sigma * (1.0 + gate * (1.0 - sigma))).astype(jnp.bfloat16)
    up_grad = (hidden_grad * silu).astype(jnp.bfloat16)
    return (hidden, gate_grad, up_grad)


def owned(array, start, size, axis):
    return lax.dynamic_slice_in_dim(array, start, size, axis)


def shards(
    layer_inputs,
    cotangent,
    gate_weight,
    up_weight,
    down_weight,
    gate_momentum,
    up_momentum,
    down_momentum,
):
    segments = lax.axis_size("segment")
    depth = segments // 2
    segment = lax.axis_index("segment")
    direction = segment % 2
    lower = direction == 0
    position = segment // 2
    gate_w = gate_weight[0]
    up_w = up_weight[0]
    down_w = down_weight[0]
    inputs = layer_inputs[0].astype(jnp.float32)
    micro, rows_dev, width = inputs.shape
    half = width // 2
    hidden_dev = gate_w.shape[1]
    total_rows = rows_dev * lax.axis_size("tp")
    inverse_norm = lax.rsqrt(jnp.mean(inputs * inputs, axis=-1, keepdims=True) + epsilon)
    exact = inputs * inverse_norm
    normed = exact.astype(jnp.bfloat16)
    entry = lax.dynamic_index_in_dim(cotangent, direction, 0, keepdims=False)
    ticks = depth + micro - 1
    wide_store = jnp.zeros((micro, total_rows, width), jnp.bfloat16)
    narrow_store = jnp.zeros((micro, total_rows, hidden_dev), jnp.bfloat16)
    extra = (wide_store, narrow_store, narrow_store, narrow_store) + (wide_store,)

    def process(tick, received, state):
        outgoing, backs, extra = state
        index = tick - position
        active = (index >= 0) & (index < micro)
        slot = jnp.clip(index, 0, micro - 1)
        local_in = jnp.where(position == 0, entry[slot], received)
        incoming_rows = lax.all_gather(local_in, "tp", axis=0, tiled=True)
        full_rows = lax.all_gather(normed[slot], "tp", axis=0, tiled=True)

        def factors():
            gate, up = project(full_rows, gate_w, up_w)
            return backward_factors(incoming_rows, gate, up, down_w)

        def resting():
            blank = jnp.zeros((total_rows, hidden_dev), jnp.bfloat16)
            return (blank, blank, blank)

        hidden, gate_grad, up_grad = lax.cond(active, factors, resting)
        count = lax.axis_size("tp") * rows_dev

        def compute():
            return contract_last(gate_grad, gate_w) + contract_last(up_grad, up_w)

        def quiet():
            return jnp.zeros((count, width), jnp.float32)

        normed_grad = lax.psum_scatter(
            lax.cond(active, compute, quiet).astype(jnp.bfloat16),
            "tp",
            scatter_dimension=0,
            tiled=True,
        ).astype(jnp.float32)
        scale = inverse_norm[slot]
        base = exact[slot]
        back = local_in.astype(jnp.float32) + scale * (
            normed_grad - base * jnp.mean(normed_grad * base, axis=-1, keepdims=True)
        )
        back = back.astype(jnp.bfloat16)
        backs = lax.dynamic_update_index_in_dim(
            backs, jnp.where(active, back, backs[slot]), slot, 0
        )
        fresh = (incoming_rows, hidden, gate_grad, up_grad) + (full_rows,)
        extra = tuple(
            (
                lax.dynamic_update_index_in_dim(
                    store, jnp.where(active, item, store[slot]), slot, 0
                )
                for store, item in zip(extra, fresh)
            )
        )
        return (back, backs, extra)

    zero_rows = jnp.zeros((rows_dev, width), jnp.bfloat16)
    state = process(
        0, zero_rows, (zero_rows, jnp.zeros((micro, rows_dev, width), jnp.bfloat16), extra)
    )

    def advance(tick, state):
        received = passed_along(state[0], "segment", 2)
        return process(tick, received, state)

    outgoing, backs, extra = lax.fori_loop(1, ticks, advance, state)
    keep_start = jnp.where(lower, 0, half)
    send_start = half - keep_start
    flat_rows = micro * total_rows
    normed_all = extra[4]
    normed_flat = normed_all.reshape(flat_rows, width)
    incoming_flat = extra[0].reshape(flat_rows, width)
    hidden_flat = extra[1].reshape(flat_rows, hidden_dev)
    gate_flat = extra[2].reshape(flat_rows, hidden_dev)
    up_flat = extra[3].reshape(flat_rows, hidden_dev)
    arrived = partner(
        (
            owned(normed_flat, send_start, half, 1),
            owned(incoming_flat, send_start, half, 1),
            hidden_flat,
            gate_flat,
            up_flat,
        ),
        "segment",
        0,
    )
    normed_keep = owned(normed_flat, keep_start, half, 1)
    incoming_keep = owned(incoming_flat, keep_start, half, 1)
    gate_share = contract_rows(normed_keep, gate_flat) + rounded(
        contract_rows(arrived[0], arrived[3])
    )
    up_share = contract_rows(normed_keep, up_flat) + rounded(contract_rows(arrived[0], arrived[4]))
    down_share = contract_rows(hidden_flat, incoming_keep) + rounded(
        contract_rows(arrived[2], arrived[1])
    )
    new_gate = (momentum_decay * gate_momentum[0] + gate_share)[None]
    new_up = (momentum_decay * up_momentum[0] + up_share)[None]
    new_down = (momentum_decay * down_momentum[0] + down_share)[None]
    return (backs[None], new_gate, new_up, new_down)


CHUNKS = 4
VMEM_LIMIT = 42 << 20


def scope(name):
    return jax.named_scope(name)


def update(d, plan, nrm, inc, hidden, gate_g, up_g, flipped, accs, news, done=None):
    _, chunks, sides, n, rows, span = nrm.shape
    total = sides * n * rows
    hid = hidden.shape[2]
    keep = d * (chunks // 2)
    step = 256

    @pl.loop(0, chunks // 2)
    def _(j):
        place = pl.ds(pl.multiple_of(j * span, span), span)
        flipped[...] = nrm[plan[0][1][0], keep + j].reshape(total, span).T

        @pl.loop(0, hid // step)
        def _(i):
            piece = pl.ds(pl.multiple_of(i * step, step), step)
            for which, ks, scale in plan:
                where = (piece, place) if which == 2 else (place, piece)
                value = accs[which][where]
                if scale:
                    value = value * momentum_decay
                for k in ks:
                    if which == 2:
                        rhs = inc[k, keep + j].reshape(total, span)
                        value = value + contract_rows(hidden[k, :, piece], rhs)
                    else:
                        grads = (gate_g, up_g)[which][k, :, piece]
                        value = value + jnp.dot(
                            flipped[...], grads, preferred_element_type=jnp.float32
                        )
                news[which][where] = value
                if done is not None:
                    done(which, where)


def apply_kernel(
    back, gate_acc, up_acc, down_acc, nrm, inc, hidden, gate_g, up_g,
    back_out, gate_out, up_out, down_out, gate_new, up_new, down_new, flipped, sems,
):
    d = lax.rem(lax.axis_index("segment"), 2)
    accs = (gate_acc, up_acc, down_acc)
    news = (gate_new, up_new, down_new)
    outs = (gate_out, up_out, down_out)
    backs = pltpu.make_async_copy(back, back_out, sems.at[3])
    backs.start()

    def done(which, where):
        pltpu.make_async_copy(
            news[which].at[where], outs[which].at[where], sems.at[which]
        ).start()

    final = nrm.shape[0] - 1
    plan = ((0, (final,), False), (1, (final,), False), (2, range(final + 1), True))
    update(d, plan, nrm, inc, hidden, gate_g, up_g, flipped, accs, news, done=done)
    for which in range(3):
        pltpu.make_async_copy(news[which], outs[which], sems.at[which]).wait()
    backs.wait()


def semaphore_keys(micro, chunks, n):
    slots = [1] + list(range(2, n, 2))
    bits = n.bit_length() - 1
    keys = []
    for k in range(micro):
        keys += [("normed", k, m) for m in slots]
        keys += [("mirror", k), ("pass", k)]
        keys += [("sum", k, chunks, b) for b in range(bits)]
        for c in range(chunks):
            keys += [("rows", k, c, m) for m in slots]
            keys += [("sum", k, c, b) for b in range(bits)]
            keys += [("mirror", k, c), ("pass", k, c), ("hop", k, c)]
            keys += [("side", k, c)] if k else []
    return {key: i for i, key in enumerate(keys)}


def relay_kernel(
    n,
    depth,
    li_hbm,
    cot_hbm,
    gate_hbm,
    up_hbm,
    down_hbm,
    gate_m,
    up_m,
    down_m,
    back_ref,
    gate_acc,
    up_acc,
    down_acc,
    nrm,
    inc,
    hidden,
    gate_g,
    up_g,
    gate_w,
    up_w,
    down_w,
    gate_t,
    up_t,
    down_t,
    li_ref,
    cot_ref,
    slope,
    silu_s,
    slant,
    grad_s,
    exact_s,
    inv_s,
    mean_s,
    parts,
    rs_recv,
    stats,
    st_recv,
    z_send,
    z_side,
    flipped,
    load_sem,
    cot_sem,
    ssem,
    rsem,
):
    micro, rows, width = li_ref.shape
    hid = down_w.shape[0]
    chunks, span = nrm.shape[1], nrm.shape[5]
    total = n * rows
    half = width // 2
    bits = n.bit_length() - 1
    top = n // 2
    s = lax.axis_index("segment")
    t = lax.axis_index("tp")
    p = lax.div(s, 2)
    d = lax.rem(s, 2)
    mirror = s + 1 - 2 * d
    first = p == 0
    early = jnp.logical_and(p > 0, p * 2 >= depth)
    last = p == depth - 1

    def flip(mask):
        value = t
        for b in range(bits):
            if mask >> b & 1:
                value = value + (1 << b) * (1 - 2 * lax.rem(lax.div(t, 1 << b), 2))
        return value

    def cols(c):
        return pl.ds(c * span, span)

    barrier = pltpu.get_barrier_semaphore()

    def greet(device):
        pl.semaphore_signal(
            barrier, inc=1, device_id=device, device_id_type=pl.DeviceIdType.MESH
        )

    for b in range(bits):
        greet({"tp": flip(1 << b)})
    greet({"segment": mirror})

    @pl.when(p > 0)
    def _():
        greet({"segment": s - 2})

    @pl.when(p < depth - 1)
    def _():
        greet({"segment": s + 2})

    sources = (li_hbm, down_hbm, gate_hbm, up_hbm, gate_m, up_m, down_m)
    targets = (li_ref, down_w, gate_w, up_w, gate_acc, up_acc, down_acc)
    loads = [
        pltpu.make_async_copy(a, b, load_sem.at[i])
        for i, (a, b) in enumerate(zip(sources, targets))
    ]

    cot_load = pltpu.make_async_copy(cot_hbm.at[d], cot_ref, cot_sem)
    def start_weights():
        for load in loads[1:4]:
            load.start()

    loads[0].start()
    pl.when(first)(cot_load.start)
    start_weights()

    keys = semaphore_keys(micro, chunks, n)

    def copy(group, key, src, dst, device):
        return pltpu.make_async_remote_copy(
            src_ref=src,
            dst_ref=dst,
            send_sem=ssem.at[group],
            recv_sem=rsem.at[keys[key]],
            device_id=device,
            device_id_type=pl.DeviceIdType.MESH,
        )

    def arrived(key, ref):
        copy(0, key, ref, ref, {"tp": flip(1)}).wait_recv()

    evens = sorted(range(2, n, 2), key=lambda m: -(m & -m))

    def spread(ref, key, m, b):
        block = ref.at[flip(m)]
        slot = m | 1 << b
        copy(0, key + (slot if b else 1,), block, block, {"tp": flip(1 << b)}).start()

    def cross(kind, k, c, m, start=True):
        if kind:
            source, target, key = inc.at[k, c, 0], inc.at[k, c, 1], ("mirror", k, c)
            source, target = source.at[flip(m)], target.at[flip(m)]
        else:
            source, target, key = nrm.at[k, :, 0, flip(m)], nrm.at[k, :, 1, flip(m)], ("mirror", k)
        copy(2, key, source, target, {"segment": mirror}).start()

    def normed_copy(k, m, b):
        block = nrm.at[k, :, 0, flip(m)]
        copy(0, ("normed", k, m | 1 << b if b else 1), block, block, {"tp": flip(1 << b)}).start()

    def normed_start(k):
        for b in reversed(range(bits)):
            normed_copy(k, 0, b)

    def normed_forward(k):
        for m in evens:
            arrived(("normed", k, m), nrm.at[k, :, 0, flip(m)])
            for b in reversed(range(bits)):
                if 1 << b < (m & -m):
                    normed_copy(k, m, b)
            cross(0, k, 0, m)

    def normed_wait(k):
        arrived(("normed", k, 1), nrm.at[k, :, 0, pl.ds(0, n // 2)])

    def rows_start(k, c):
        for b in reversed(range(bits)):
            spread(inc.at[k, c, 0], ("rows", k, c), 0, b)

    def rows_forward(k, c):
        for m in evens:
            arrived(("rows", k, c, m), inc.at[k, c, 0, flip(m)])
            for b in reversed(range(bits)):
                if 1 << b < (m & -m):
                    spread(inc.at[k, c, 0], ("rows", k, c), m, b)
            cross(1, k, c, m)

    def rows_wait(k, c):
        arrived(("rows", k, c, 1), inc.at[k, c, 0, pl.ds(0, n // 2)])

    def normed_pass(k):
        arrived(("mirror", k), nrm.at[k, :, 1, pl.ds(0, n // 2)])
        for m in range(0, n, 2):
            block = nrm.at[k, :, 1, flip(m)]
            copy(2, ("pass", k), block, block, {"tp": flip(1)}).start()

    def rows_pass(k, c):
        arrived(("mirror", k, c), inc.at[k, c, 1, pl.ds(0, n // 2)])
        for m in range(0, n, 2):
            block = inc.at[k, c, 1, flip(m)]
            copy(2, ("pass", k, c), block, block, {"tp": flip(1)}).start()

    def turn(source, target):
        step = 256

        @pl.loop(0, source.shape[1] // step)
        def _(j):
            piece = pl.ds(pl.multiple_of(j * step, step), step)
            target[piece, :] = source[:, piece].T

    def forward(side, k, also=False):
        step = min(256, hid)
        here = pl.ds(side * total, total)

        @pl.loop(0, hid // step)
        def _(j):
            piece = pl.ds(pl.multiple_of(j * step, step), step)
            g = jnp.zeros((total, step), jnp.float32)
            u = jnp.zeros((total, step), jnp.float32)
            for c in range(chunks):
                lhs = nrm[k, c, side].reshape(total, span)
                g = g + jnp.dot(lhs, gate_w[cols(c), piece], preferred_element_type=jnp.float32)
                u = u + jnp.dot(lhs, up_w[cols(c), piece], preferred_element_type=jnp.float32)
            sigma = jax.nn.sigmoid(g)
            sl = g * sigma
            sp = u * sigma * (1.0 + g * (1.0 - sigma))
            hidden[k, here, piece] = (sl * u).astype(jnp.bfloat16)
            slope[k, here, piece] = sp
            silu_s[k, here, piece] = sl
            if side == 0:
                slant[k, :, piece] = sp * g + sl * u
            if also:
                up_t[piece, :] = up_w[:, piece].T

    def accumulate(side, k, c):
        lhs = inc[k, c, side].reshape(total, span)
        value = jnp.dot(lhs, down_t[cols(c), :], preferred_element_type=jnp.float32)
        if c:
            value = grad_s[side] + value
        grad_s[side] = value

    def factors(side, k):
        here = pl.ds(side * total, total)
        step = min(128, hid)
        sums = jnp.zeros((total, step), jnp.float32)
        for j in range(hid // step):
            piece = pl.ds(j * step, step)
            grad = grad_s[side, :, piece]
            gate_g[k, here, piece] = (grad * slope[k, here, piece]).astype(jnp.bfloat16)
            up_g[k, here, piece] = (grad * silu_s[k, here, piece]).astype(jnp.bfloat16)
            if side == 0:
                sums = sums + grad * slant[k, :, piece]
        if side == 0:
            stats[k] = sums.reshape(n, rows, step)

    def partial_grads(k, c):
        gg = gate_g[k, :total, :]
        ug = up_g[k, :total, :]
        part = jnp.dot(gg, gate_t[:, cols(c)], preferred_element_type=jnp.float32)
        part = part + jnp.dot(ug, up_t[:, cols(c)], preferred_element_type=jnp.float32)
        parts[k, c] = part.astype(jnp.bfloat16).reshape(n, rows, span)

    def rs_refs(k, c):
        if c == chunks:
            return stats.at[k], st_recv.at[k]
        return parts.at[k, c], rs_recv.at[k, c]

    def rs_round(k, c, b):
        source, target = rs_refs(k, c)
        for m in range(0, n, 1 << (b + 1)):
            q = m | 1 << b
            if b:
                value = source[flip(q)].astype(jnp.float32)
                for lower in range(b):
                    value = value + target[q | 1 << lower].astype(jnp.float32)
                source[flip(q)] = value.astype(source.dtype)
            copy(
                1 if c == chunks else 0,
                ("sum", k, c, b),
                source.at[flip(q)],
                target.at[q],
                {"tp": flip(1 << b)},
            ).start()

    def rs_wait(k, c, b):
        arrived(("sum", k, c, b), rs_refs(k, c)[1].at[pl.ds(0, n >> (b + 1))])

    def rs_total(k, c):
        source, target = rs_refs(k, c)
        value = source[t].astype(jnp.float32)
        for b in range(bits):
            value = value + target[1 << b].astype(jnp.float32)
        return value

    def receive(k, c):
        arrived(("hop", k, c), inc.at[k, c, 0, t])
        if k == 0:
            rows_start(k, c)
        else:
            for b in range(bits - 1):
                spread(inc.at[k, c, 0], ("rows", k, c), 0, b)
        cross(1, k, c, 0)

    def detour(k, c):
        @pl.when(p < depth - 1)
        def _():
            arrived(("side", k, c), z_side.at[k - 1, c])
            target = inc.at[k, c, 0, flip(top)]
            device = {"segment": s + 2}
            copy(4, ("rows", k, c, top), z_side.at[k - 1, c], target, device).start()

    def reduce(k, c):
        for b in range(1, bits):
            rs_wait(k, c, b - 1)
            rs_round(k, c, b)

    def finish(k, c):
        if c == 0:
            rs_wait(k, chunks, bits - 1)
            sums = rs_total(k, chunks)
            mean_s[k] = jnp.sum(sums, axis=-1, keepdims=True) * (1.0 / width)
        rs_wait(k, c, bits - 1)
        value = rs_total(k, c)
        own = inc[k, c, 0, t].astype(jnp.float32)
        back = own + inv_s[k] * (value - exact_s[k, c] * mean_s[k])
        back = back.astype(jnp.bfloat16)
        z_send[k, c] = back

        @pl.when(p < depth - 1)
        def _():
            target = inc.at[k, c, 0, t]
            copy(3, ("hop", k, c), z_send.at[k, c], target, {"segment": s + 2}).start()
            if k:
                target = z_side.at[k - 1, c]
                copy(4, ("side", k, c), z_send.at[k, c], target, {"tp": flip(top)}).start()

        back_ref[k, :, cols(c)] = back

    loads[0].wait()
    for k in range(micro):
        x = li_ref[k].astype(jnp.float32)
        inv = lax.rsqrt(jnp.mean(x * x, axis=-1, keepdims=True) + epsilon)
        inv_s[k] = inv
        for c in range(chunks):
            exact = x[:, c * span : (c + 1) * span] * inv
            exact_s[k, c] = exact
            nrm[k, c, 0, t] = exact.astype(jnp.bfloat16)

    peers = bits + 1 + jnp.minimum(p, 1) + jnp.minimum(depth - 1 - p, 1)
    with scope("barrier"):
        pl.semaphore_wait(barrier, peers)

    normed_start(0)
    for k in range(micro):
        cross(0, k, 0, 0)

    def mirror_forward():
        for k in range(micro):
            normed_pass(k)
        for k in range(micro):
            arrived(("pass", k), nrm.at[k, :, 1, pl.ds(0, n // 2)])
            forward(1, k)

    def cot_start(k):
        @pl.when(first)
        def _():
            for c in range(chunks):
                rows_start(k, c)
            for c in range(chunks):
                cross(1, k, c, 0)

    with scope("t1"):
        loads[1].wait()
        turn(down_w, down_t)

    @pl.when(first)
    def _():
        cot_load.wait()
        for k in range(micro):
            for c in range(chunks):
                inc[k, c, 0, t] = cot_ref[k, :, cols(c)]

    cot_start(0)
    with scope("t2"):
        loads[2].wait()
        loads[3].wait()
        for load in loads[4:]:
            load.start()
        turn(gate_w, gate_t)
    for k in range(1, micro):
        normed_start(k)
    for k in range(1, micro):
        cot_start(k)
    with scope("nf0"):
        normed_forward(0)
    with scope("nw0"):
        normed_wait(0)
    with scope("fw0"):
        forward(0, 0, True)

    def project_all():
        for k in range(1, micro):
            normed_forward(k)
            normed_wait(k)
            forward(0, k)

    with scope("fw1"):
        pl.when(jnp.logical_not(first))(project_all)
    with scope("mf"):
        pl.when(early)(mirror_forward)

    def side_gather(k, c):
        arrived(("pass", k, c), inc.at[k, c, 1, pl.ds(0, n // 2)])
        accumulate(1, k, c)

    def gather(k, c):
        rows_wait(k, c)
        accumulate(0, k, c)

    def factor(k):
        factors(0, k)
        rs_round(k, chunks, 0)

    def partial(k, c):
        partial_grads(k, c)
        rs_round(k, c, 0)

    def change(k):
        if k == 0:
            for load in loads[4:]:
                load.wait()
        accs = (gate_acc, up_acc, down_acc)
        plan = ((0, (k,), k == 0), (1, (k,), k == 0))
        update(d, plan, nrm, inc, hidden, gate_g, up_g, flipped, accs, accs)

    def project(k):
        normed_wait(k)
        forward(0, k)

    def mirrored():
        pl.when(jnp.logical_not(early))(mirror_forward)

    def traced(name, step):
        return step

    R, F, K = traced("R", receive), traced("F", rows_forward), traced("K", gather)
    E, P = traced("E", factor), traced("P", partial)
    S, Q = traced("S", lambda k: reduce(k, chunks)), traced("Q", reduce)
    G, H, X = traced("G", finish), traced("H", detour), traced("X", rows_pass)
    N, W, V = traced("N", normed_forward), traced("W", project), traced("V", mirrored)
    m, M = traced("m", side_gather), traced("M", lambda k: factors(1, k))
    U = traced("U", change)

    def each(*pairs):
        for c in range(chunks):
            for step, k in pairs:
                step(k, c)

    def products(k, between=None, fill=None):
        for c in range(chunks):
            if c == 2:
                S(k)
            P(k, c)
            if c >= 2:
                Q(k, c - 2)
                if fill is not None:
                    fill(k - 1, c - 2)
        if between is not None:
            between(1)
        for c in range(chunks - 2, chunks):
            Q(k, c)
            if fill is not None:
                fill(k - 1, c)

    def finals():
        each((X, 0))
        each((G, 1))
        each((H, 1))
        each((X, 1))
        V()
        each((m, 0))
        M(0)
        U(0)
        each((m, 1))
        M(1)

    def play_first():
        each((F, 0))
        each((K, 0))
        E(0)
        products(0, between=N)
        each((F, 1))
        W(1)
        each((G, 0), (K, 1))
        E(1)
        products(1)
        finals()

    def play_middle():
        each((R, 0))
        each((F, 0))
        each((K, 0))
        E(0)
        products(0)
        each((R, 1))
        each((F, 1), (G, 0))
        each((K, 1))
        E(1)
        products(1)
        finals()

    def play_last():
        each((R, 0))
        each((F, 0))
        each((K, 0))
        E(0)
        products(0)
        each((X, 0))
        each((R, 1))
        for c in range(chunks - 1):
            m(0, c)
        for c in range(chunks):
            if c == chunks - 2:
                m(0, chunks - 1)
            if c == chunks - 1:
                M(0)
            F(1, c)
        each((K, 1))
        E(1)
        products(1, fill=G)
        each((X, 1))
        U(0)
        each((m, 1))
        M(1)
        each((G, 1))

    pl.when(first)(play_first)
    pl.when(jnp.logical_not(jnp.logical_or(first, last)))(play_middle)
    pl.when(last)(play_last)

    block = rows * span
    sizes = (
        micro * chunks * (n - 1) * 3 * block,
        micro * (n - 1) * rows * 128,
        micro * chunks * 2 * n * block,
        micro * chunks * block,
        2 * (micro - 1) * chunks * block,
        micro * chunks * (n - 1) * 3 * block - (micro - 1) * chunks * block,
    )

    def sends_done(group, ref, size=None):
        view = ref.at[pl.ds(0, sizes[group if size is None else size] // ref.shape[1])]
        copy(group, ("normed", 0, 1), view, view, {"tp": flip(1)}).wait_send()

    with scope("sends"):
        pl.when(first)(lambda: sends_done(0, gate_w))
        pl.when(jnp.logical_not(first))(lambda: sends_done(0, gate_w, 5))
        sends_done(1, gate_acc)
        sends_done(2, gate_w)

        @pl.when(p < depth - 1)
        def _():
            sends_done(3, gate_w)
            sends_done(4, gate_w)


def relayed(
    segments,
    n,
    layer_inputs,
    cotangent,
    gate_weight,
    up_weight,
    down_weight,
    gate_momentum,
    up_momentum,
    down_momentum,
):
    _, micro, rows, width = layer_inputs.shape
    hid = gate_weight.shape[2]
    half = width // 2
    chunks = CHUNKS
    span = width // chunks
    total = n * rows
    hbm = pl.BlockSpec(memory_space=pl.ANY)
    bf, f32 = jnp.bfloat16, jnp.float32
    ends = pl.pallas_call(
        functools.partial(relay_kernel, n, segments // 2),
        name="relay",
        out_shape=(
            pltpu.VMEM((micro, rows, width), bf),
            pltpu.VMEM((half, hid), f32),
            pltpu.VMEM((half, hid), f32),
            pltpu.VMEM((hid, half), f32),
            pltpu.VMEM((micro, chunks, 2, n, rows, span), bf),
            pltpu.VMEM((micro, chunks, 2, n, rows, span), bf),
            pltpu.VMEM((micro, 2 * total, hid), bf),
            pltpu.VMEM((micro, 2 * total, hid), bf),
            pltpu.VMEM((micro, 2 * total, hid), bf),
        ),
        in_specs=[hbm] * 8,
        scratch_shapes=[
            pltpu.VMEM((width, hid), bf),
            pltpu.VMEM((width, hid), bf),
            pltpu.VMEM((hid, width), bf),
            pltpu.VMEM((hid, width), bf),
            pltpu.VMEM((hid, width), bf),
            pltpu.VMEM((width, hid), bf),
            pltpu.VMEM((micro, rows, width), bf),
            pltpu.VMEM((micro, rows, width), bf),
            pltpu.VMEM((micro, 2 * total, hid), f32),
            pltpu.VMEM((micro, 2 * total, hid), f32),
            pltpu.VMEM((micro, total, hid), f32),
            pltpu.VMEM((2, total, hid), f32),
            pltpu.VMEM((micro, chunks, rows, span), f32),
            pltpu.VMEM((micro, rows, 1), f32),
            pltpu.VMEM((micro, rows, 1), f32),
            pltpu.VMEM((micro, chunks, n, rows, span), bf),
            pltpu.VMEM((micro, chunks, n, rows, span), bf),
            pltpu.VMEM((micro, n, rows, 128), f32),
            pltpu.VMEM((micro, n, rows, 128), f32),
            pltpu.VMEM((micro, chunks, rows, span), bf),
            pltpu.VMEM((micro - 1, chunks, rows, span), bf),
            pltpu.VMEM((span, 2 * total), bf),
            pltpu.SemaphoreType.DMA((7,)),
            pltpu.SemaphoreType.DMA(()),
            pltpu.SemaphoreType.DMA((5,)),
            pltpu.SemaphoreType.DMA((len(semaphore_keys(micro, chunks, n)),)),
        ],
        compiler_params=pltpu.CompilerParams(
            collective_id=0, has_side_effects=True, vmem_limit_bytes=VMEM_LIMIT
        ),
    )(
        layer_inputs[0],
        cotangent,
        gate_weight[0],
        up_weight[0],
        down_weight[0],
        gate_momentum[0],
        up_momentum[0],
        down_momentum[0],
    )
    vmem = pl.BlockSpec(memory_space=pltpu.VMEM)
    back, new_gate, new_up, new_down = pl.pallas_call(
        apply_kernel,
        name="apply",
        out_shape=(
            jax.ShapeDtypeStruct((micro, rows, width), bf),
            jax.ShapeDtypeStruct((half, hid), f32),
            jax.ShapeDtypeStruct((half, hid), f32),
            jax.ShapeDtypeStruct((hid, half), f32),
        ),
        in_specs=[vmem] * 9,
        out_specs=(hbm,) * 4,
        scratch_shapes=[
            pltpu.VMEM((half, hid), f32),
            pltpu.VMEM((half, hid), f32),
            pltpu.VMEM((hid, half), f32),
            pltpu.VMEM((span, 2 * total), bf),
            pltpu.SemaphoreType.DMA((4,)),
        ],
        compiler_params=pltpu.CompilerParams(vmem_limit_bytes=13 << 20),
    )(*ends)
    return (back[None], new_gate[None], new_up[None], new_down[None])


def choose(segments, n, *arrays):
    rows = arrays[0].shape[2]
    if rows % 16 == 0 and n == 4 and segments > 2 and arrays[0].shape[1] == 2:
        return relayed(segments, n, *arrays)
    return shards(*arrays)


def solution(mesh):
    body = functools.partial(choose, mesh.shape["segment"], mesh.shape["tp"])
    return jax.shard_map(
        body,
        mesh=mesh,
        in_specs=(
            P("segment", None, "tp", None),
            P(None, None, "tp", None),
            P("segment", None, "tp"),
            P("segment", None, "tp"),
            P("segment", "tp", None),
            P("segment", None, "tp"),
            P("segment", None, "tp"),
            P("segment", "tp", None),
        ),
        out_specs=(
            P("segment", None, "tp", None),
            P("segment", None, "tp"),
            P("segment", None, "tp"),
            P("segment", "tp", None),
        ),
        check_vma=False,
    )
```
